32 devices in a mesh: expert: 16 (over z, y, core), tensor: 2 (over x).
Axes of the slice: x: 2, y: 2, z: 4, core: 2. Of those that a mesh axis runs over, the one named last changes fastest.
Arguments:
- tokens: bfloat16 [512, 7168], P('expert'), may hold values from -6 to 6
- cotangent: bfloat16 [512, 7168], P('expert'), may hold values from -1.5 to 1.5
- gate_weights: bfloat16 [512, 8], P('expert'), may hold values from 0.019897461 to 0.5
- route_slots: int32 [512, 8], P('expert'), may hold values from 0 to 15, all different within a row; in each aligned block of 32 rows (0 to 31, 32 to 63, ...) at most 24 rows name the same one
- replica_owner: int32 [2], replicated, may hold values from 0 to 13, as said below
- w_gate: bfloat16 [16, 7168, 1024], P('expert', None, 'tensor'), as said below
- w_up: bfloat16 [16, 7168, 1024], P('expert', None, 'tensor'), as said below
- w_down: bfloat16 [16, 7168, 1024], P('expert', None, 'tensor'), as said below
Outputs:
- input_grads: bfloat16 [512, 7168], P('expert', 'tensor')
- gate_grads: bfloat16 [512, 8], P('expert')
- expert_grads: bfloat16 [14, 7168, 3, 1024], P(None, 'expert', None, 'tensor')
The draws below stay inside these ranges and needn't reach their ends.
Inputs may be any that keep to these rules, and one draw needn't show every extreme that they name: `route_slots`: in each block of 32 tokens no slot is named by more than 24 entries, a bound that some block reaches; a token names 8 different slots. `replica_owner`: numbers of experts; one expert may own several replicas, and a replica slot's weights equal its expert's. `w_gate`: slot 14 + r holds the same matrix as slot replica_owner[r]. `w_up`: slot 14 + r holds the same matrix as slot replica_owner[r]. `w_down`: slot 14 + r holds the same matrix as slot replica_owner[r].
All inputs are finite; a program needn't handle non-finite values.
Results may differ from the reference program's by a relative error of at most 0.012.
Values may be sent and summed in bfloat16 or wider, within the bound.
No kernel may reach another device: no remote copies, remote signals or barrier semaphores. Data moves between devices by JAX's collectives and lax.ppermute only.
A program may use at most 128 MiB of HBM per device.

```python
import math
import jax
import jax.numpy as jnp
import numpy as np
from jax import lax

D = 7168
TOP = 8
FF = 1024
TOK_DEV = 32
TOKENS = 512
ROWS = 384
CAP = 24
REPLICAS = 2
LOGICAL = 14
N_EXPERT = 16
N_TENSOR = 2


def replica_table(key):
    hot_expert = jax.random.randint(jax.random.fold_in(key, 5), (1,), 0, LOGICAL, dtype=jnp.int32)
    spread = jax.random.randint(jax.random.fold_in(key, 6), (REPLICAS,), 0, LOGICAL, dtype=jnp.int32)
    coins = jax.random.randint(jax.random.fold_in(key, 7), (REPLICAS,), 0, 2, dtype=jnp.int32)
    owners = jnp.where(coins == 1, hot_expert, spread).astype(jnp.int32)
    last_mark = jnp.arange(REPLICAS, dtype=jnp.int32) == REPLICAS - 1
    owners = jnp.where(last_mark, jnp.int32(LOGICAL - 1), owners).astype(jnp.int32)
    return jnp.concatenate([jnp.arange(LOGICAL, dtype=jnp.int32), owners])


def tied_weights(key, salt, fan_in):
    slot_table = replica_table(key)
    shape = (LOGICAL, D, FF)
    base = jax.random.normal(jax.random.fold_in(key, salt), shape, jnp.float32)
    return (base[slot_table] * fan_in ** (-0.5)).astype(jnp.bfloat16)


def draw_replica_owner(key, part):
    return replica_table(key)[LOGICAL:]


def draw_w_gate(key, part):
    return tied_weights(key, 11, D)


def draw_w_up(key, part):
    return tied_weights(key, 12, D)


def draw_w_down(key, part):
    return tied_weights(key, 13, FF)


def block_levels(key, dims, shards, least, largest):
    gain = 1.0
    for dim, blocks in shards:
        heights = jax.random.uniform(jax.random.fold_in(jax.random.fold_in(key, 6), dim), (blocks,), jnp.float32, least / len(shards), largest / len(shards))
        gain = gain * jnp.repeat(jnp.exp(heights), dims[dim] // blocks).reshape((-1,) + (1,) * (len(dims) - 1 - dim))
    return gain


def shared_out(rng, own, number, rows, amount, top, reach, lean):
    order = jax.random.permutation(rng, amount)
    packed, common = load_shares(amount, rows * top, reach, lean, True), load_shares(amount, rows * top, reach, lean, False)
    places = jnp.arange(amount)

    def named(lengths, turn):
        used = int((lengths > 0).sum())
        fixed = max(1, used // 4)
        moved = fixed + (places - fixed + turn * (used - fixed)) % max(1, amount - fixed)
        return jnp.zeros((amount,), jnp.int32).at[order[jnp.where(places < fixed, places, moved)]].set(jnp.asarray(lengths, jnp.int32))

    lengths = jnp.where(number % 4 == 0, named(packed, number // 4), named(common, number - number // 4 - 1))
    mixed = jax.random.permutation(jax.random.fold_in(own, 3), amount)
    donor, receiver = mixed[0:amount // 2 * 2:2], mixed[1:amount // 2 * 2:2]
    room = jnp.minimum(lengths[donor] - 1, reach - lengths[receiver]) // 2
    room = jnp.where((donor == order[0]) | (receiver == order[0]) | (lengths[receiver] == 0), 0, jnp.maximum(room, 0))
    moved = jax.random.randint(jax.random.fold_in(own, 4), (amount // 2,), 0, 1 << 20) % (room + 1)
    lengths = lengths.at[donor].add(-moved).at[receiver].add(moved)
    labels = jnp.searchsorted(jnp.cumsum(lengths), jnp.arange(rows * top), side="right").astype(jnp.int32)
    listing = labels.reshape(top, rows).T
    listing = listing[jax.random.permutation(jax.random.fold_in(own, 1), rows)]
    turn = jax.random.randint(jax.random.fold_in(own, 2), (rows, 1), 0, top)
    return jnp.take_along_axis(listing, (jnp.arange(top)[None, :] + turn) % top, axis=1)


def load_shares(number_of, total, reach, lean, full):
    loads = [(1 << 20) // math.isqrt(standing ** lean) + 1 for standing in range(1, number_of + 1)]
    largest = reach if full else min(reach, max(-(-total // number_of), total * loads[0] // sum(loads)))
    least = 1 if total - largest >= number_of - 1 else 0
    counts, rest = [largest] + [least] * (number_of - 1), total - largest - least * (number_of - 1)
    while rest > 0:
        candidates = [i for i in range(1, number_of) if counts[i] < largest] or [i for i in range(1, number_of) if counts[i] < reach]
        whole, budget = sum([loads[i] for i in candidates]), rest
        for i in candidates:
            more = min(reach - counts[i], max(1, budget * loads[i] // whole), rest)
            counts[i] = counts[i] + more
            rest = rest - more
    return np.array(counts)


def gaussian(rng, extent, deviation, reach, cuts=(), kind=jnp.bfloat16):
    drawn = jax.random.normal(rng, extent, jnp.float32) * deviation
    if len(cuts) > 0:
        drawn = block_levels(rng, extent, cuts, -0.22, 0.18) * drawn
    return jnp.clip(drawn, min=-reach, max=reach).astype(kind)


def setup_inputs(seed: int = 0) -> dict:
    arg_keys = jax.random.split(jax.random.key(seed), 9)
    tokens = gaussian(arg_keys[0], (TOKENS, D), 1.0, 6.0, ((0, 16),))
    cotangent = gaussian(arg_keys[1], (TOKENS, D), 0.25, 1.5, ((0, 16),))
    gate_weights = jnp.clip(jnp.exp(math.log(0.5) - 3.224016 * jax.random.uniform(arg_keys[2], (TOKENS, TOP), jnp.float32) ** block_levels(arg_keys[2], (TOKENS, TOP), ((0, 16),), -0.2, 0.2)), 0.019897461, 0.5).astype(jnp.bfloat16)
    route_slots_keys = jax.random.split(jax.random.fold_in(arg_keys[3], 1), TOKENS // TOK_DEV)
    route_slots_turns = jax.random.permutation(jax.random.fold_in(arg_keys[3], 3), TOKENS // TOK_DEV)
    route_slots = jax.vmap(lambda own, number: shared_out(jax.random.fold_in(arg_keys[3], 2), own, number, TOK_DEV, N_EXPERT, TOP, CAP, 2))(route_slots_keys, route_slots_turns).reshape((TOKENS, TOP))
    replica_owner = draw_replica_owner(jax.random.fold_in(arg_keys[8], 71), 0)
    w_gate = draw_w_gate(jax.random.fold_in(arg_keys[8], 71), 0)
    w_up = draw_w_up(jax.random.fold_in(arg_keys[8], 71), 0)
    w_down = draw_w_down(jax.random.fold_in(arg_keys[8], 71), 0)
    return {"tokens": tokens, "cotangent": cotangent, "gate_weights": gate_weights, "route_slots": route_slots, "replica_owner": replica_owner, "w_gate": w_gate, "w_up": w_up, "w_down": w_down}


def dispatch_targets(route_block, slot_total, capacity):
    flat_ids = route_block.reshape(-1)
    one_hot = (flat_ids[:, None] == jnp.arange(slot_total, dtype=jnp.int32)[None, :]).astype(jnp.int32)
    earlier = jnp.cumsum(one_hot, axis=0) - 1
    position = jnp.sum(one_hot * earlier, axis=1)
    return (flat_ids * capacity + position).reshape(route_block.shape).astype(jnp.int32)


def reference(tokens, cotangent, gate_weights, route_slots, replica_owner, w_gate, w_up, w_down):
    token_blocks = tokens.reshape(N_EXPERT, TOK_DEV, D).astype(jnp.float32)
    cot_blocks = cotangent.reshape(N_EXPERT, TOK_DEV, D).astype(jnp.float32)
    route_blocks = route_slots.reshape(N_EXPERT, TOK_DEV, TOP)
    gate_blocks = gate_weights.reshape(N_EXPERT, TOK_DEV, TOP).astype(jnp.float32)
    targets = jax.vmap(lambda block: dispatch_targets(block, N_EXPERT, CAP))(route_blocks)
    matches = targets[:, None, :, :] == jnp.arange(ROWS, dtype=jnp.int32)[None, :, None, None]
    select = jnp.any(matches, axis=3)
    select_f = select.astype(jnp.float32)
    gate_send = jnp.sum(jnp.where(matches, gate_blocks[:, None, :, :], 0.0), axis=(2, 3)).astype(jnp.bfloat16)
    quarter = FF // N_TENSOR

    def expert_step(slot):
        picked = lax.dynamic_slice_in_dim(select_f, slot * CAP, CAP, 1)
        x_rows = jnp.einsum("bct,btd->bcd", picked, token_blocks).reshape(ROWS, D).astype(jnp.bfloat16)
        dy_rows = jnp.einsum("bct,btd->bcd", picked, cot_blocks).reshape(ROWS, D).astype(jnp.bfloat16)
        g_rows = lax.dynamic_slice_in_dim(gate_send, slot * CAP, CAP, 1).reshape(ROWS)
        gate_mat = w_gate[slot]
        up_mat = w_up[slot]
        down_mat = w_down[slot]
        gate_proj = jnp.dot(x_rows, gate_mat, preferred_element_type=jnp.float32)
        up_proj = jnp.dot(x_rows, up_mat, preferred_element_type=jnp.float32)
        sigmoid_gate = jax.nn.sigmoid(gate_proj)
        activated = gate_proj * sigmoid_gate
        hidden = (activated * up_proj).astype(jnp.bfloat16)
        expert_out = jnp.dot(hidden, down_mat.T, preferred_element_type=jnp.float32)
        row_score = jnp.sum(dy_rows.astype(jnp.float32) * expert_out, axis=1).astype(jnp.bfloat16)
        scaled = (g_rows.astype(jnp.float32)[:, None] * dy_rows.astype(jnp.float32)).astype(jnp.bfloat16)
        hidden_grad = jnp.dot(scaled, down_mat, preferred_element_type=jnp.float32)
        up_grad = (hidden_grad * activated).astype(jnp.bfloat16)
        pre_grad = (hidden_grad * up_proj * sigmoid_gate * (1.0 + gate_proj * (1.0 - sigmoid_gate))).astype(jnp.bfloat16)
        grad_gate = jnp.dot(x_rows.T, pre_grad, preferred_element_type=jnp.float32)
        grad_up = jnp.dot(x_rows.T, up_grad, preferred_element_type=jnp.float32)
        grad_down = jnp.dot(scaled.T, hidden, preferred_element_type=jnp.float32)
        slot_grads = jnp.stack([grad_gate, grad_up, grad_down], axis=1).astype(jnp.bfloat16)
        input_sum = jnp.zeros((ROWS, D), jnp.float32)
        for block in range(N_TENSOR):
            lower = block * quarter
            upper = lower + quarter
            term = jnp.dot(pre_grad[:, lower:upper], gate_mat[:, lower:upper].T, preferred_element_type=jnp.float32)
            term = term + jnp.dot(up_grad[:, lower:upper], up_mat[:, lower:upper].T, preferred_element_type=jnp.float32)
            input_sum = input_sum + lax.optimization_barrier(term.astype(jnp.bfloat16)).astype(jnp.float32)
        return row_score, input_sum.astype(jnp.bfloat16), slot_grads

    replica_out = lax.map(expert_step, LOGICAL + jnp.arange(REPLICAS, dtype=jnp.int32))

    def primary_step(expert):
        row_score, row_input, slot_grads = expert_step(expert)
        owned = (replica_owner == expert)[:, None, None, None]
        total = slot_grads.astype(jnp.float32) + jnp.sum(jnp.where(owned, replica_out[2].astype(jnp.float32), 0.0), axis=0)
        return row_score, row_input, total.astype(jnp.bfloat16)

    primary_out = lax.map(primary_step, jnp.arange(LOGICAL, dtype=jnp.int32))
    score_all = jnp.concatenate([primary_out[0], replica_out[0]], axis=0)
    input_all = jnp.concatenate([primary_out[1], replica_out[1]], axis=0)

    def return_block(source):
        back_rows = lax.dynamic_slice_in_dim(input_all, source * CAP, CAP, 1).reshape(ROWS, D)
        back_score = lax.dynamic_slice_in_dim(score_all, source * CAP, CAP, 1).reshape(ROWS)
        select_block = select[source].astype(jnp.bfloat16)
        grad_rows = lax.dot_general(select_block, back_rows, ((((0,), (0,))), ((), ())), preferred_element_type=jnp.float32)
        grad_gate = back_score[targets[source]]
        return grad_rows.astype(jnp.bfloat16), grad_gate

    grad_rows, grad_gate = lax.map(return_block, jnp.arange(N_EXPERT, dtype=jnp.int32))
    return grad_rows.reshape(TOKENS, D), grad_gate.reshape(TOKENS, TOP), primary_out[2]
```

```python
import jax
import jax.numpy as jnp
from jax import lax
from jax.experimental import pallas as pl
from jax.experimental.pallas import tpu as pltpu
from jax.sharding import PartitionSpec as P


BF = jnp.bfloat16
F32 = jnp.float32
LANES = 128
ANY = pl.BlockSpec(memory_space=pl.ANY)


def split_axis(total):
    cores = 2
    chips = total // cores
    b = 1
    while b * b * 4 <= chips:
        b *= 2
    return chips // b, b, cores


def block_of(size, most):
    return max(n for n in range(LANES, most + 1, LANES) if size % n == 0)


class Grid:
    def __init__(self):
        self.total = lax.axis_size("expert")
        self.sizes = split_axis(self.total)
        self.me = lax.axis_index("expert")
        _, nb, nc = self.sizes
        self.pos = (self.me // (nb * nc), (self.me // nc) % nb, self.me % nc)
        self.parts = lax.axis_size("tensor")
        self.part = lax.axis_index("tensor")

    def flat(self, a, b, c):
        _, nb, nc = self.sizes
        return (a * nb + b) * nc + c

    def shift(self, value, axis, step):
        pairs = []
        for a in range(self.sizes[0]):
            for b in range(self.sizes[1]):
                for c in range(self.sizes[2]):
                    src = [a, b, c]
                    src[axis] = (src[axis] + step) % self.sizes[axis]
                    pairs.append((self.flat(*src), self.flat(a, b, c)))
        return lax.ppermute(value, "expert", pairs)

    def tensor_shift(self, value, step):
        n = self.parts
        return lax.ppermute(value, "tensor", [((i + step) % n, i) for i in range(n)])

    def ids(self):
        na, nb, nc = self.sizes
        a, b, c = self.pos
        places = [(da, db, dc) for dc in range(nc) for db in range(nb) for da in range(na)]
        return jnp.stack(
            [self.flat((a + da) % na, (b + db) % nb, (c + dc) % nc) for da, db, dc in places]
        ).astype(jnp.int32)

    def gather_small(self, own):
        out = own[None]
        for axis in range(3):
            parts = [out] + [self.shift(out, axis, k) for k in range(1, self.sizes[axis])]
            out = jnp.concatenate(parts)
        return out

    def gather(self, own):
        na, nb, nc = self.sizes
        line = [own]
        for k in range(1, na):
            line.append(self.shift(own, 0, k))
        plane = list(line)
        for j in range(1, nb):
            for k in range(na):
                plane.append(self.shift(line[k], 1, j))
        out = list(plane)
        for d in range(1, nc):
            for piece in plane:
                out.append(self.shift(piece, 2, d))
        return out

    def gather_rows(self, own):
        na, nb, nc = self.sizes
        part = own.shape[1] // self.parts
        mine = lax.dynamic_slice_in_dim(own, self.part * part, part, 1)
        plane = [(0, None, own)]
        line = []
        for k in range(1, na):
            line.append(self.shift(mine, 0, k))
        for j in range(1, nb):
            plane.append((j * na, None, self.shift(own, 1, j)))
        groups = [(1, jnp.concatenate(line))]
        for j in range(1, nb):
            groups.append((j * na + 1, self.shift(groups[0][1], 1, j)))
        for block, piece in groups:
            plane.append((block, 0, piece))
            for h in range(1, self.parts):
                plane.append((block, h, self.tensor_shift(piece, h)))
        out = list(plane)
        for d in range(1, nc):
            for block, h, piece in plane:
                out.append((d * na * nb + block, h, self.shift(piece, 2, d)))
        return out


def load_rows(where, at_ref, piece_refs, whole, sem, parts, tok):
    part = whole.shape[1] // parts
    copies = []
    for n, ((block, h), ref) in enumerate(zip(where, piece_refs)):
        rows = pl.ds(block * tok, ref.shape[0])
        if h is None:
            to = whole.at[rows, :]
        else:
            start = pl.multiple_of(((at_ref[0] + h) % parts) * part, LANES)
            to = whole.at[rows, pl.ds(start, part)]
        copies.append(pltpu.make_async_copy(ref, to, sem.at[n]))
    for copy in copies:
        copy.start()
    for copy in copies:
        copy.wait()


def pick_matrix(place, rows):
    ids = lax.broadcasted_iota(jnp.int32, (rows, place.shape[1]), 0)
    return jnp.where(ids == place, 1.0, 0.0).astype(BF)


def window_of(width, depth):
    return min(width, -(-(depth + LANES - 1) // LANES) * LANES)


def gate_kernel(where, parts, tok, at_ref, wg_ref, wu_ref, gate_ref, place_ref, *refs):
    count = len(where)
    pieces = refs[:count]
    proj_ref, up_ref, down_ref, window_ref, whole, acc, sem, wsem = refs[count:]
    j = pl.program_id(0)
    block = wg_ref.shape[0]
    window = window_ref.shape[1]

    @pl.when(j == 0)
    def _():
        load_rows(where, at_ref, pieces, whole, sem, parts, tok)

    cols = pl.ds(pl.multiple_of(j * block, LANES), block)
    x = whole[:, cols]
    g = jnp.dot(x, wg_ref[...], preferred_element_type=F32)
    u = jnp.dot(x, wu_ref[...], preferred_element_type=F32)

    @pl.when(j == 0)
    def _():
        acc[0] = g
        acc[1] = u

    @pl.when(j > 0)
    def _():
        acc[0] += g
        acc[1] += u

    @pl.when(j == pl.num_programs(0) - 1)
    def _():
        start = pl.multiple_of(at_ref[1], LANES)
        copy = pltpu.make_async_copy(whole.at[:, pl.ds(start, window)], window_ref, wsem)
        copy.start()
        proj, up = acc[0], acc[1]
        proj_ref[...] = proj
        up_ref[...] = up
        hidden = proj * jax.nn.sigmoid(proj) * up
        weighted = (gate_ref[...] * hidden).astype(BF)
        pick = pick_matrix(place_ref[...], down_ref.shape[0])
        down_ref[...] = jnp.dot(pick, weighted, preferred_element_type=F32).astype(BF)
        copy.wait()


def down_kernel(where, parts, tok, at_ref, wd_ref, gate_ref, place_ref, proj_ref, up_ref, *refs):
    count = len(where)
    pieces = refs[:count]
    pre_ref, upg_ref, send_ref, score_ref, window_ref, whole, acc, sem, wsem = refs[count:]
    j = pl.program_id(0)
    block = wd_ref.shape[0]
    window = window_ref.shape[1]

    @pl.when(j == 0)
    def _():
        load_rows(where, at_ref, pieces, whole, sem, parts, tok)

    cols = pl.ds(pl.multiple_of(j * block, LANES), block)
    d = jnp.dot(whole[:, cols], wd_ref[...], preferred_element_type=F32)

    @pl.when(j == 0)
    def _():
        acc[...] = d

    @pl.when(j > 0)
    def _():
        acc[...] += d

    @pl.when(j == pl.num_programs(0) - 1)
    def _():
        start = pl.multiple_of(at_ref[1], LANES)
        copy = pltpu.make_async_copy(whole.at[:, pl.ds(start, window)], window_ref, wsem)
        copy.start()
        proj, up, dy_down = proj_ref[...], up_ref[...], acc[...]
        sigma = jax.nn.sigmoid(proj)
        activated = proj * sigma
        score = jnp.sum(activated * up * dy_down, axis=1, keepdims=True)
        lane = lax.broadcasted_iota(jnp.int32, score_ref.shape, 1)
        score_ref[...] = jnp.where(lane == at_ref[2], score, 0.0).astype(BF)
        grad = gate_ref[...] * dy_down
        upg = (grad * activated).astype(BF)
        pre = (grad * up * sigma * (1.0 + proj * (1.0 - sigma))).astype(BF)
        pre_ref[...] = pre
        upg_ref[...] = upg
        rows, hidden = send_ref.shape[0], pre.shape[1]
        pick = pick_matrix(place_ref[...], rows)
        send_ref[:, :hidden] = jnp.dot(pick, pre, preferred_element_type=F32).astype(BF)
        send_ref[:, hidden:] = jnp.dot(pick, upg, preferred_element_type=F32).astype(BF)
        copy.wait()


def full(shape):
    return pl.BlockSpec(shape, lambda *_: (0,) * len(shape))


def forward_call(kernel, at, weights, small, pieces, outs, accs, width, rows_all, depth, parts, tok):
    where = [(block, h) for block, h, _ in pieces]
    values = [piece for _, _, piece in pieces]
    hidden = weights[0].shape[1]
    block = block_of(width, 1024)
    window = window_of(width, depth)
    body = lambda *refs: kernel(where, parts, tok, *refs)
    return pl.pallas_call(
        body,
        grid_spec=pltpu.PrefetchScalarGridSpec(
            num_scalar_prefetch=1,
            grid=(width // block,),
            in_specs=[pl.BlockSpec((block, hidden), lambda j, at: (j, 0)) for _ in weights]
            + [full(value.shape) for value in small]
            + [ANY for _ in values],
            out_specs=[full(out.shape) for out in outs] + [ANY],
            scratch_shapes=[
                pltpu.VMEM((rows_all, width), BF),
                pltpu.VMEM(accs, F32),
                pltpu.SemaphoreType.DMA((len(values),)),
                pltpu.SemaphoreType.DMA,
            ],
        ),
        out_shape=list(outs) + [jax.ShapeDtypeStruct((rows_all, window), BF)],
    )(at, *weights, *small, *values)


def input_kernel(index_ref, pre_ref, up_ref, score_ref, wg_ref, wu_ref, out_ref):
    dims = (((1,), (1,)), ((), ()))
    acc = lax.dot_general(pre_ref[...], wg_ref[...], dims, preferred_element_type=F32)
    acc = acc + lax.dot_general(up_ref[...], wu_ref[...], dims, preferred_element_type=F32)
    rows = out_ref.shape[2]
    block = wg_ref.shape[0]
    j = pl.program_id(1)
    part = out_ref.shape[3] - score_ref.shape[1]
    cols = pl.ds(pl.multiple_of(j * block, LANES), block)
    for c in range(out_ref.shape[0]):
        out_ref[c, 0, :, cols] = acc[c * rows : (c + 1) * rows].astype(BF)

    @pl.when(j == 0)
    def _():
        for c in range(out_ref.shape[0]):
            out_ref[c, 0, :, part:] = score_ref[c * rows : (c + 1) * rows, :]


def input_parts(grid, pre, up, score, w_gate, w_up):
    tokens, hidden = pre.shape
    width = w_gate.shape[0]
    parts, cores = grid.parts, grid.sizes[2]
    part = width // parts
    block = block_of(part, 512)
    steps = part // block
    index = grid.part.astype(jnp.int32).reshape(1)

    def weight_map(h, j, idx):
        return (((idx[0] + h) % parts) * steps + j, 0)

    return pl.pallas_call(
        input_kernel,
        grid_spec=pltpu.PrefetchScalarGridSpec(
            num_scalar_prefetch=1,
            grid=(parts, steps),
            in_specs=[
                full((tokens, hidden)),
                full((tokens, hidden)),
                full(score.shape),
                pl.BlockSpec((block, hidden), weight_map),
                pl.BlockSpec((block, hidden), weight_map),
            ],
            out_specs=pl.BlockSpec(
                (cores, 1, tokens // cores, part + LANES), lambda h, j, idx: (0, h, 0, 0)
            ),
        ),
        out_shape=jax.ShapeDtypeStruct((cores, parts, tokens // cores, part + LANES), BF),
    )(index, pre, up, score, w_gate, w_up)


def pick_kernel(place_ref, x_ref, dy_ref, xo_ref, dyo_ref):
    pick = pick_matrix(place_ref[0], xo_ref.shape[2])
    dims = (((1,), (1,)), ((), ()))
    xo_ref[0] = lax.dot_general(x_ref[...], pick, dims, preferred_element_type=F32).astype(BF)
    dyo_ref[0] = lax.dot_general(dy_ref[...], pick, dims, preferred_element_type=F32).astype(BF)


def picked(place, x_t, dy_t, rows):
    slots, tokens = place.shape
    depth = x_t.shape[0]
    out = jax.ShapeDtypeStruct((slots, depth, rows), BF)
    return pl.pallas_call(
        pick_kernel,
        grid=(slots,),
        in_specs=[
            pl.BlockSpec((1, 1, tokens), lambda s: (s, 0, 0)),
            full(x_t.shape),
            full(dy_t.shape),
        ],
        out_specs=[pl.BlockSpec((1, depth, rows), lambda s: (s, 0, 0))] * 2,
        out_shape=[out, out],
    )(place.reshape(slots, 1, tokens), x_t, dy_t)


def expert_kernel(slots, replicas, table_ref, rows_ref, *refs):
    pieces = refs[:slots]
    out_ref, left, right, acc, sem_l, sem_r = refs[-6:]
    e = pl.program_id(0)
    experts = slots - replicas
    count = out_ref.shape[1]
    hidden = out_ref.shape[3]

    def left_copy(i):
        return pltpu.make_async_copy(rows_ref.at[i], left.at[i], sem_l.at[i])

    def right_copy(i, at):
        return pltpu.make_async_copy(pieces[i], right.at[at], sem_r.at[at])

    @pl.when(e == 0)
    def _():
        for i in range(slots):
            left_copy(i).start()
            right_copy(i, i).start()
        for r in range(replicas):
            i = table_ref[experts + r]
            left_copy(i).wait()
            right_copy(0, i).wait()

    at = table_ref[e]
    left_copy(at).wait()
    right_copy(0, at).wait()
    rows = left[at]
    for j in range(count):
        acc[j] = jnp.dot(
            rows, right[at, :, j * hidden : (j + 1) * hidden], preferred_element_type=F32
        )
    for r in range(replicas):

        @pl.when(table_ref[slots + r] == e)
        def _(r=r):
            i = table_ref[experts + r]
            for j in range(count):
                acc[j] += jnp.dot(
                    left[i], right[i, :, j * hidden : (j + 1) * hidden], preferred_element_type=F32
                )

    for j in range(count):
        out_ref[0, j] = acc[j].astype(BF)


def expert_sums(table, rows, pieces, first, count, total, previous, replicas):
    slots, depth, n = rows.shape
    experts = slots - replicas
    hidden = pieces[0].shape[1] // count
    operands = [rows] + list(pieces)
    aliases = {}
    if previous is not None:
        operands.append(previous)
        aliases = {len(operands): 0}
    return pl.pallas_call(
        lambda *refs: expert_kernel(slots, replicas, *refs),
        grid_spec=pltpu.PrefetchScalarGridSpec(
            num_scalar_prefetch=1,
            grid=(experts,),
            in_specs=[ANY for _ in operands],
            out_specs=pl.BlockSpec(
                (1, count, depth, hidden), lambda e, t: (e, first // count, 0, 0)
            ),
            scratch_shapes=[
                pltpu.VMEM((slots, depth, n), BF),
                pltpu.VMEM((slots, n, count * hidden), BF),
                pltpu.VMEM((count, depth, hidden), F32),
                pltpu.SemaphoreType.DMA((slots,)),
                pltpu.SemaphoreType.DMA((slots,)),
            ],
        ),
        out_shape=jax.ShapeDtypeStruct((experts, total, depth, hidden), BF),
        input_output_aliases=aliases,
    )(table, *operands)


def after(value, *others):
    return lax.optimization_barrier((value, *others))[0]


def per_device(tokens, cotangent, gate_weights, route_slots, replica_owner, w_gate, w_up, w_down):
    grid = Grid()
    slots = grid.total
    na, nb, nc = grid.sizes
    tok, width = tokens.shape
    top = route_slots.shape[1]
    rows = tok * top * 3 // 2
    replicas = replica_owner.shape[0]
    wg, wu, wd = w_gate[0], w_up[0], w_down[0]
    hidden = wg.shape[1]
    all_tok = tok * slots
    depth = width // slots
    part = width // grid.parts

    meta = jnp.concatenate(
        [route_slots.astype(BF), gate_weights, jnp.zeros((tok, LANES - 2 * top), BF)], axis=1
    )
    meta_all = grid.gather_small(meta).reshape(all_tok, LANES)
    x_pieces = grid.gather_rows(tokens)
    dy_pieces = grid.gather_rows(cotangent)

    ids = grid.ids()
    routes = meta_all[:, :top].astype(jnp.int32)
    gates = meta_all[:, top : 2 * top].astype(F32)
    token_ids = (ids[:, None] * tok + jnp.arange(tok, dtype=jnp.int32)[None, :]).reshape(-1)
    named = jnp.any(routes[None, :, :] == ids[:, None, None], axis=2)
    before = (token_ids[:, None] < token_ids[None, :]).astype(BF)
    place = jnp.dot(named.astype(BF), before, preferred_element_type=F32).astype(jnp.int32)
    place = jnp.where(named, place, -1)
    gate = jnp.sum(jnp.where(routes == ids[0], gates, 0.0), axis=1)[:, None]

    first = grid.me * depth
    window = window_of(width, depth)
    start = jnp.minimum(first // LANES * LANES, width - window)
    at = jnp.stack([grid.part, start, grid.me]).astype(jnp.int32)
    square = jax.ShapeDtypeStruct((all_tok, hidden), F32)
    square_b = jax.ShapeDtypeStruct((all_tok, hidden), BF)
    proj, up_proj, down, x_window = forward_call(
        gate_kernel,
        at,
        [wg, wu],
        [gate, place[:1]],
        x_pieces,
        [square, square, jax.ShapeDtypeStruct((rows, hidden), BF)],
        (2, all_tok, hidden),
        width,
        all_tok,
        depth,
        grid.parts,
        tok,
    )
    down_all = grid.gather(down)
    pre, upg, send, score, dy_window = forward_call(
        down_kernel,
        at,
        [wd],
        [gate, place[:1], proj, up_proj],
        dy_pieces,
        [
            square_b,
            square_b,
            jax.ShapeDtypeStruct((rows, 2 * hidden), BF),
            jax.ShapeDtypeStruct((all_tok, LANES), BF),
        ],
        (all_tok, hidden),
        width,
        all_tok,
        depth,
        grid.parts,
        tok,
    )
    send_all = grid.gather(send)

    parts = input_parts(grid, pre, upg, score, wg, wu)
    kept = parts[0].astype(F32)
    for k in range(1, nc):
        kept = kept + grid.shift(parts[k], 2, -k).astype(F32)
    kept = kept.astype(BF)
    terms = [kept[0]] + [grid.tensor_shift(kept[k], -k) for k in range(1, grid.parts)]
    if grid.parts > 2:
        terms = list(jnp.roll(jnp.stack(terms)[::-1], grid.part + 1, axis=0))
    total = terms[0].astype(F32)
    for term in terms[1:]:
        total = total + term.astype(F32)
    total = total.astype(BF).reshape(nb, na, tok, part + LANES)
    line = total[0].astype(F32)
    for k in range(1, nb):
        line = line + grid.shift(total[k], 1, -k).astype(F32)
    line = line.astype(BF)
    last = line[0].astype(F32)
    for k in range(1, na):
        last = last + grid.shift(line[k], 0, -k).astype(F32)
    input_grads = last[:, :part].astype(BF)
    lane = jnp.arange(LANES, dtype=jnp.int32)
    own_routes = route_slots[:, :, None] == lane[None, None, :]
    gate_grads = jnp.sum(jnp.where(own_routes, last[:, None, part:], 0.0), axis=2).astype(BF)

    x_window, dy_window = after(x_window, parts), after(dy_window, parts)
    x_t = lax.dynamic_slice_in_dim(x_window, first - start, depth, 1).T
    dy_t = lax.dynamic_slice_in_dim(dy_window, first - start, depth, 1).T
    x_pick, dy_pick = picked(place, x_t, dy_t, rows)
    spot = jnp.sum(
        jnp.where(
            ids[None, :] == jnp.arange(slots, dtype=jnp.int32)[:, None],
            jnp.arange(slots, dtype=jnp.int32)[None, :],
            0,
        ),
        axis=1,
    )
    table = jnp.concatenate([spot, replica_owner]).astype(jnp.int32)
    out = expert_sums(table, dy_pick, down_all, 2, 1, 3, None, replicas)
    out = expert_sums(table, x_pick, send_all, 0, 2, 3, out, replicas)
    return input_grads, gate_grads, jnp.transpose(out, (0, 2, 1, 3))


def solution(mesh):
    in_specs = (
        P("expert", None),
        P("expert", None),
        P("expert", None),
        P("expert", None),
        P(),
        P("expert", None, "tensor"),
        P("expert", None, "tensor"),
        P("expert", None, "tensor"),
    )
    out_specs = (P("expert", "tensor"), P("expert", None), P(None, "expert", None, "tensor"))

    return jax.shard_map(
        per_device, mesh=mesh, in_specs=in_specs, out_specs=out_specs, check_vma=False
    )
```

```python
import jax
import jax.numpy as jnp
from jax import lax
from jax.experimental import pallas as pl
from jax.experimental.pallas import tpu as pltpu
from jax.sharding import PartitionSpec as P


BF = jnp.bfloat16
F32 = jnp.float32
LANES = 128
ANY = pl.BlockSpec(memory_space=pl.ANY)


def split_axis(total):
    cores = 2
    chips = total // cores
    b = 1
    while b * b * 4 <= chips:
        b *= 2
    return chips // b, b, cores


def block_of(size, most):
    return max(n for n in range(LANES, most + 1, LANES) if size % n == 0)


def nearest_steps(size):
    return sorted(range(1, size), key=lambda k: (min(k, size - k), k))


class Grid:
    def __init__(self):
        self.total = lax.axis_size("expert")
        self.sizes = split_axis(self.total)
        self.me = lax.axis_index("expert")
        _, nb, nc = self.sizes
        self.pos = (self.me // (nb * nc), (self.me // nc) % nb, self.me % nc)
        self.parts = lax.axis_size("tensor")
        self.part = lax.axis_index("tensor")

    def flat(self, a, b, c):
        _, nb, nc = self.sizes
        return (a * nb + b) * nc + c

    def shift(self, value, axis, step):
        pairs = []
        for a in range(self.sizes[0]):
            for b in range(self.sizes[1]):
                for c in range(self.sizes[2]):
                    src = [a, b, c]
                    src[axis] = (src[axis] + step) % self.sizes[axis]
                    pairs.append((self.flat(*src), self.flat(a, b, c)))
        return lax.ppermute(value, "expert", pairs)

    def tensor_shift(self, value, step):
        n = self.parts
        return lax.ppermute(value, "tensor", [((i + step) % n, i) for i in range(n)])

    def ids(self):
        na, nb, nc = self.sizes
        a, b, c = self.pos
        places = [(da, db, dc) for dc in range(nc) for db in range(nb) for da in range(na)]
        return jnp.stack(
            [self.flat((a + da) % na, (b + db) % nb, (c + dc) % nc) for da, db, dc in places]
        ).astype(jnp.int32)

    def gather_small(self, own):
        out = own[None]
        for axis in range(3):
            parts = [out]
            for k in range(1, self.sizes[axis]):
                parts.append(self.shift(out, axis, k))
            out = jnp.concatenate(parts)
        return out

    def nearest(self):
        return nearest_steps(self.sizes[0])

    def gather(self, own):
        na, nb, nc = self.sizes
        line = {0: own}
        for k in self.nearest():
            line[k] = self.shift(own, 0, k)
        plane = [line[k] for k in range(na)]
        for j in range(1, nb):
            for k in range(na):
                plane.append(self.shift(line[k], 1, j))
        out = list(plane)
        for d in range(1, nc):
            for piece in plane:
                out.append(self.shift(piece, 2, d))
        return out

    def gather_rows(self, own, lent):
        na, nb, nc = self.sizes
        width = own.shape[1]
        keep = width - (self.parts - 1) * lent
        mine = lax.dynamic_slice_in_dim(own, self.part * lent, keep, 1)
        lend = self.part * ((width - lent) // (self.parts - 1) - lent)
        plane = [(0, None, own)]
        swaps = [(0, None, own)]
        line = {}
        for k in self.nearest():
            line[k] = self.shift(mine, 0, k)
        for j in range(1, nb):
            piece = self.shift(own, 1, j)
            plane.append((j * na, None, piece))
            swaps.append((j * na, None, piece))
        for j in range(nb):
            row = dict(line)
            if j > 0:
                for k in self.nearest():
                    row[k] = self.shift(line[k], 1, j)
            kinds = [row]
            for h in range(1, self.parts):
                lent_row = {}
                for k in self.nearest():
                    piece = row[k]
                    if lent < keep:
                        piece = lax.dynamic_slice_in_dim(piece, lend, lent, 1)
                    lent_row[k] = self.tensor_shift(piece, h)
                kinds.append(lent_row)
            for h, pieces in enumerate(kinds):
                plane += [(j * na + k, h, pieces[k]) for k in range(1, na)]
                group = jnp.concatenate([pieces[k] for k in range(1, na)])
                swaps.append((j * na + 1, h, group))
        out = list(plane)
        for d in range(1, nc):
            for block, h, piece in swaps:
                out.append((d * na * nb + block, h, self.shift(piece, 2, d)))
        return out


def load_rows(where, at_ref, piece_refs, whole, sem, parts, tok):
    width = whole.shape[1]
    copies = []
    for n, ((block, h), ref) in enumerate(zip(where, piece_refs)):
        rows = pl.ds(block * tok, ref.shape[0])
        if h is None:
            to = whole.at[rows, :]
        else:
            cols = ref.shape[1]
            step = (width - cols) // (parts - 1)
            start = pl.multiple_of(((at_ref[0] + h) % parts) * step, LANES)
            to = whole.at[rows, pl.ds(start, cols)]
        copies.append(pltpu.make_async_copy(ref, to, sem.at[n]))
    for copy in copies:
        copy.start()
    for copy in copies:
        copy.wait()


def pick_matrix(place, rows):
    ids = lax.broadcasted_iota(jnp.int32, (rows, place.shape[1]), 0)
    return jnp.where(ids == place, 1.0, 0.0).astype(BF)


def window_of(width, depth):
    return min(width, -(-(depth + LANES - 1) // LANES) * LANES)


def gate_kernel(where, parts, tok, at_ref, wg_ref, wu_ref, gate_ref, place_ref, *refs):
    count = len(where)
    pieces = refs[:count]
    proj_ref, up_ref, down_ref, window_ref, whole, acc, sem, wsem = refs[count:]
    j = pl.program_id(0)
    block = wg_ref.shape[0]
    window = window_ref.shape[1]

    @pl.when(j == 0)
    def _():
        load_rows(where, at_ref, pieces, whole, sem, parts, tok)

    cols = pl.ds(pl.multiple_of(j * block, LANES), block)
    x = whole[:, cols]
    g = jnp.dot(x, wg_ref[...], preferred_element_type=F32)
    u = jnp.dot(x, wu_ref[...], preferred_element_type=F32)

    @pl.when(j == 0)
    def _():
        acc[0] = g
        acc[1] = u

    @pl.when(j > 0)
    def _():
        acc[0] += g
        acc[1] += u

    @pl.when(j == pl.num_programs(0) - 1)
    def _():
        start = pl.multiple_of(at_ref[1], LANES)
        copy = pltpu.make_async_copy(whole.at[:, pl.ds(start, window)], window_ref, wsem)
        copy.start()
        proj, up = acc[0], acc[1]
        proj_ref[...] = proj
        up_ref[...] = up
        hidden = proj * jax.nn.sigmoid(proj) * up
        weighted = (gate_ref[...] * hidden).astype(BF)
        pick = pick_matrix(place_ref[...], down_ref.shape[0])
        down_ref[...] = jnp.dot(pick, weighted, preferred_element_type=F32).astype(BF)
        copy.wait()


def down_kernel(where, parts, tok, at_ref, wd_ref, gate_ref, place_ref, proj_ref, up_ref, *refs):
    count = len(where)
    pieces = refs[:count]
    pre_ref, upg_ref, pre_rows_ref, upg_rows_ref, score_ref, window_ref, whole, acc, sem, wsem = refs[count:]
    j = pl.program_id(0)
    block = wd_ref.shape[0]
    window = window_ref.shape[1]

    @pl.when(j == 0)
    def _():
        load_rows(where, at_ref, pieces, whole, sem, parts, tok)

    cols = pl.ds(pl.multiple_of(j * block, LANES), block)
    d = jnp.dot(whole[:, cols], wd_ref[...], preferred_element_type=F32)

    @pl.when(j == 0)
    def _():
        acc[...] = d

    @pl.when(j > 0)
    def _():
        acc[...] += d

    @pl.when(j == pl.num_programs(0) - 1)
    def _():
        start = pl.multiple_of(at_ref[1], LANES)
        copy = pltpu.make_async_copy(whole.at[:, pl.ds(start, window)], window_ref, wsem)
        copy.start()
        proj, up, dy_down = proj_ref[...], up_ref[...], acc[...]
        sigma = jax.nn.sigmoid(proj)
        activated = proj * sigma
        score = jnp.sum(activated * up * dy_down, axis=1, keepdims=True)
        lane = lax.broadcasted_iota(jnp.int32, score_ref.shape, 1)
        score_ref[...] = jnp.where(lane == at_ref[2], score, 0.0).astype(BF)
        grad = gate_ref[...] * dy_down
        upg = (grad * activated).astype(BF)
        pre = (grad * up * sigma * (1.0 + proj * (1.0 - sigma))).astype(BF)
        pre_ref[...] = pre
        upg_ref[...] = upg
        pick = pick_matrix(place_ref[...], pre_rows_ref.shape[0])
        pre_rows_ref[...] = jnp.dot(pick, pre, preferred_element_type=F32).astype(BF)
        upg_rows_ref[...] = jnp.dot(pick, upg, preferred_element_type=F32).astype(BF)
        copy.wait()


def full(shape):
    return pl.BlockSpec(shape, lambda *_: (0,) * len(shape))


def forward_call(kernel, at, weights, small, pieces, outs, accs, width, rows_all, depth, parts, tok):
    where = [(block, h) for block, h, _ in pieces]
    values = [piece for _, _, piece in pieces]
    hidden = weights[0].shape[1]
    block = block_of(width, 1024)
    window = window_of(width, depth)
    body = lambda *refs: kernel(where, parts, tok, *refs)
    return pl.pallas_call(
        body,
        grid_spec=pltpu.PrefetchScalarGridSpec(
            num_scalar_prefetch=1,
            grid=(width // block,),
            in_specs=[pl.BlockSpec((block, hidden), lambda j, at: (j, 0)) for _ in weights]
            + [full(value.shape) for value in small]
            + [ANY for _ in values],
            out_specs=[full(out.shape) for out in outs] + [ANY],
            scratch_shapes=[
                pltpu.VMEM((rows_all, width), BF),
                pltpu.VMEM(accs, F32),
                pltpu.SemaphoreType.DMA((len(values),)),
                pltpu.SemaphoreType.DMA,
            ],
        ),
        out_shape=list(outs) + [jax.ShapeDtypeStruct((rows_all, window), BF)],
    )(at, *weights, *small, *values)


def input_kernel(index_ref, pre_ref, up_ref, score_ref, wg_ref, wu_ref, out_ref):
    dims = (((1,), (1,)), ((), ()))
    acc = lax.dot_general(pre_ref[...], wg_ref[...], dims, preferred_element_type=F32)
    acc = acc + lax.dot_general(up_ref[...], wu_ref[...], dims, preferred_element_type=F32)
    rows = out_ref.shape[1]
    block = wg_ref.shape[0]
    j = pl.program_id(0)
    part = out_ref.shape[2] - score_ref.shape[1]
    cols = pl.ds(pl.multiple_of(j * block, LANES), block)
    for c in range(out_ref.shape[0]):
        out_ref[c, :, cols] = acc[c * rows : (c + 1) * rows].astype(BF)

    @pl.when(j == 0)
    def _():
        for c in range(out_ref.shape[0]):
            out_ref[c, :, part:] = score_ref[c * rows : (c + 1) * rows, :]


def input_part(grid, h, pre, up, score, w_gate, w_up):
    tokens, hidden = pre.shape
    width = w_gate.shape[0]
    parts, cores = grid.parts, grid.sizes[2]
    part = width // parts
    block = block_of(part, 512)
    steps = part // block
    index = ((grid.part + h) % parts).astype(jnp.int32).reshape(1)
    weight = pl.BlockSpec((block, hidden), lambda j, idx: (idx[0] * steps + j, 0))
    shape = (cores, tokens // cores, part + LANES)
    return pl.pallas_call(
        input_kernel,
        grid_spec=pltpu.PrefetchScalarGridSpec(
            num_scalar_prefetch=1,
            grid=(steps,),
            in_specs=[
                full((tokens, hidden)),
                full((tokens, hidden)),
                full(score.shape),
                weight,
                weight,
            ],
            out_specs=full(shape),
        ),
        out_shape=jax.ShapeDtypeStruct(shape, BF),
    )(index, pre, up, score, w_gate, w_up)


def pick_kernel(place_ref, x_ref, dy_ref, xo_ref, dyo_ref):
    pick = pick_matrix(place_ref[0], xo_ref.shape[2])
    dims = (((1,), (1,)), ((), ()))
    xo_ref[0] = lax.dot_general(x_ref[...], pick, dims, preferred_element_type=F32).astype(BF)
    dyo_ref[0] = lax.dot_general(dy_ref[...], pick, dims, preferred_element_type=F32).astype(BF)


def picked(place, x_t, dy_t, rows):
    slots, tokens = place.shape
    depth = x_t.shape[0]
    out = jax.ShapeDtypeStruct((slots, depth, rows), BF)
    return pl.pallas_call(
        pick_kernel,
        grid=(slots,),
        in_specs=[
            pl.BlockSpec((1, 1, tokens), lambda s: (s, 0, 0)),
            full(x_t.shape),
            full(dy_t.shape),
        ],
        out_specs=[pl.BlockSpec((1, depth, rows), lambda s: (s, 0, 0))] * 2,
        out_shape=[out, out],
    )(place.reshape(slots, 1, tokens), x_t, dy_t)


def expert_kernel(slots, replicas, table_ref, rows_ref, *refs):
    pieces = refs[:slots]
    out_ref, left, right, acc, sem_l, sem_r = refs[-6:]
    e = pl.program_id(0)
    experts = slots - replicas
    count = out_ref.shape[1]
    hidden = out_ref.shape[3]

    def left_copy(i):
        return pltpu.make_async_copy(rows_ref.at[i], left.at[i], sem_l.at[i])

    def right_copy(i, at):
        return pltpu.make_async_copy(pieces[i], right.at[at], sem_r.at[at])

    @pl.when(e == 0)
    def _():
        def issue(n, carry):
            i = table_ref[jnp.where(n < replicas, experts + n, n - replicas)]
            left_copy(i).start()
            for k in range(slots):

                @pl.when(i == k)
                def _(k=k):
                    right_copy(k, k).start()

            return carry

        lax.fori_loop(0, slots, issue, 0)
        for r in range(replicas):
            i = table_ref[experts + r]
            left_copy(i).wait()
            right_copy(0, i).wait()

    at = table_ref[e]
    left_copy(at).wait()
    right_copy(0, at).wait()
    rows = left[at]
    for j in range(count):
        acc[j] = jnp.dot(
            rows, right[at, :, j * hidden : (j + 1) * hidden], preferred_element_type=F32
        )
    for r in range(replicas):

        @pl.when(table_ref[slots + r] == e)
        def _(r=r):
            i = table_ref[experts + r]
            for j in range(count):
                acc[j] += jnp.dot(
                    left[i], right[i, :, j * hidden : (j + 1) * hidden], preferred_element_type=F32
                )

    for j in range(count):
        out_ref[0, j] = acc[j].astype(BF)


def expert_sums(table, rows, pieces, first, count, total, previous, replicas):
    slots, depth, n = rows.shape
    experts = slots - replicas
    hidden = pieces[0].shape[1] // count
    operands = [rows] + list(pieces)
    aliases = {}
    if previous is not None:
        operands.append(previous)
        aliases = {len(operands): 0}
    return pl.pallas_call(
        lambda *refs: expert_kernel(slots, replicas, *refs),
        grid_spec=pltpu.PrefetchScalarGridSpec(
            num_scalar_prefetch=1,
            grid=(experts,),
            in_specs=[ANY for _ in operands],
            out_specs=pl.BlockSpec(
                (1, count, depth, hidden), lambda e, t: (e, first // count, 0, 0)
            ),
            scratch_shapes=[
                pltpu.VMEM((slots, depth, n), BF),
                pltpu.VMEM((slots, n, count * hidden), BF),
                pltpu.VMEM((count, depth, hidden), F32),
                pltpu.SemaphoreType.DMA((slots,)),
                pltpu.SemaphoreType.DMA((slots,)),
            ],
        ),
        out_shape=jax.ShapeDtypeStruct((experts, total, depth, hidden), BF),
        input_output_aliases=aliases,
    )(table, *operands)


def lent_columns(width, parts, sevenths):
    if parts > 2:
        return width // parts
    return width * sevenths // 7 // LANES * LANES


def after(value, *others):
    return lax.optimization_barrier((value, *others))[0]


def per_device(tokens, cotangent, gate_weights, route_slots, replica_owner, w_gate, w_up, w_down):
    grid = Grid()
    slots = grid.total
    na, nb, nc = grid.sizes
    tok, width = tokens.shape
    top = route_slots.shape[1]
    rows = tok * top * 3 // 2
    replicas = replica_owner.shape[0]
    wg, wu, wd = w_gate[0], w_up[0], w_down[0]
    hidden = wg.shape[1]
    all_tok = tok * slots
    depth = width // slots
    part = width // grid.parts

    meta = jnp.concatenate(
        [route_slots.astype(BF), gate_weights, jnp.zeros((tok, LANES - 2 * top), BF)], axis=1
    )
    meta_all = grid.gather_small(meta).reshape(all_tok, LANES)
    x_pieces = grid.gather_rows(tokens, width // grid.parts)
    dy_pieces = grid.gather_rows(cotangent, lent_columns(width, grid.parts, 2))

    ids = grid.ids()
    routes = meta_all[:, :top].astype(jnp.int32)
    gates = meta_all[:, top : 2 * top].astype(F32)
    token_ids = (ids[:, None] * tok + jnp.arange(tok, dtype=jnp.int32)[None, :]).reshape(-1)
    named = jnp.any(routes[None, :, :] == ids[:, None, None], axis=2)
    before = (token_ids[:, None] < token_ids[None, :]).astype(BF)
    place = jnp.dot(named.astype(BF), before, preferred_element_type=F32).astype(jnp.int32)
    place = jnp.where(named, place, -1)
    gate = jnp.sum(jnp.where(routes == ids[0], gates, 0.0), axis=1)[:, None]

    first = grid.me * depth
    window = window_of(width, depth)
    start = jnp.minimum(first // LANES * LANES, width - window)
    at = jnp.stack([grid.part, start, grid.me]).astype(jnp.int32)
    square = jax.ShapeDtypeStruct((all_tok, hidden), F32)
    square_b = jax.ShapeDtypeStruct((all_tok, hidden), BF)
    proj, up_proj, down, x_window = forward_call(
        gate_kernel,
        at,
        [wg, wu],
        [gate, place[:1]],
        x_pieces,
        [square, square, jax.ShapeDtypeStruct((rows, hidden), BF)],
        (2, all_tok, hidden),
        width,
        all_tok,
        depth,
        grid.parts,
        tok,
    )
    down_all = grid.gather(down)
    pre, upg, pre_rows, upg_rows, score, dy_window = forward_call(
        down_kernel,
        at,
        [wd],
        [gate, place[:1], proj, up_proj],
        dy_pieces,
        [
            square_b,
            square_b,
            jax.ShapeDtypeStruct((rows, hidden), BF),
            jax.ShapeDtypeStruct((rows, hidden), BF),
            jax.ShapeDtypeStruct((all_tok, LANES), BF),
        ],
        (all_tok, hidden),
        width,
        all_tok,
        depth,
        grid.parts,
        tok,
    )
    pre_all = grid.gather(pre_rows)
    upg_all = grid.gather(upg_rows)

    terms = {}
    for h in [*range(1, grid.parts), 0]:
        share = input_part(grid, h, pre, upg, score, wg, wu)
        total = share[0].astype(F32)
        for k in range(1, nc):
            total = total + grid.shift(share[k], 2, -k).astype(F32)
        terms[h] = total.astype(BF)
        if h > 0:
            terms[h] = grid.tensor_shift(terms[h], -h)
    terms = [terms[h] for h in range(grid.parts)]
    if grid.parts > 2:
        terms = list(jnp.roll(jnp.stack(terms)[::-1], grid.part + 1, axis=0))
    total = terms[0].astype(F32)
    for term in terms[1:]:
        total = total + term.astype(F32)
    total = total.astype(BF).reshape(nb, na, tok, part + LANES)
    line = total[0].astype(F32)
    for k in range(1, nb):
        line = line + grid.shift(total[k], 1, -k).astype(F32)
    line = line.astype(BF)
    last = line[0].astype(F32)
    for k in range(1, na):
        last = last + grid.shift(line[k], 0, -k).astype(F32)
    input_grads = last[:, :part].astype(BF)
    lane = jnp.arange(LANES, dtype=jnp.int32)
    own_routes = route_slots[:, :, None] == lane[None, None, :]
    gate_grads = jnp.sum(jnp.where(own_routes, last[:, None, part:], 0.0), axis=2).astype(BF)

    x_window, dy_window = after(x_window, share), after(dy_window, share)
    x_t = lax.dynamic_slice_in_dim(x_window, first - start, depth, 1).T
    dy_t = lax.dynamic_slice_in_dim(dy_window, first - start, depth, 1).T
    x_pick, dy_pick = picked(place, x_t, dy_t, rows)
    spot = jnp.sum(
        jnp.where(
            ids[None, :] == jnp.arange(slots, dtype=jnp.int32)[:, None],
            jnp.arange(slots, dtype=jnp.int32)[None, :],
            0,
        ),
        axis=1,
    )
    table = jnp.concatenate([spot, replica_owner]).astype(jnp.int32)
    out = expert_sums(table, dy_pick, down_all, 2, 1, 3, None, replicas)
    out = expert_sums(table, x_pick, pre_all, 0, 1, 3, out, replicas)
    out = expert_sums(table, x_pick, upg_all, 1, 1, 3, out, replicas)
    return input_grads, gate_grads, jnp.transpose(out, (0, 2, 1, 3))


def solution(mesh):
    in_specs = (
        P("expert", None),
        P("expert", None),
        P("expert", None),
        P("expert", None),
        P(),
        P("expert", None, "tensor"),
        P("expert", None, "tensor"),
        P("expert", None, "tensor"),
    )
    out_specs = (P("expert", "tensor"), P("expert", None), P(None, "expert", None, "tensor"))

    return jax.shard_map(
        per_device, mesh=mesh, in_specs=in_specs, out_specs=out_specs, check_vma=False
    )
```

```python
import jax
import jax.numpy as jnp
from jax import lax
from jax.experimental import pallas as pl
from jax.experimental.pallas import tpu as pltpu
from jax.sharding import PartitionSpec as P


BF = jnp.bfloat16
F32 = jnp.float32
LANES = 128
ANY = pl.BlockSpec(memory_space=pl.ANY)


def split_axis(total):
    cores = 2
    chips = total // cores
    b = 1
    while b * b * 4 <= chips:
        b *= 2
    return chips // b, b, cores


def block_of(size, most):
    return max(n for n in range(LANES, most + 1, LANES) if size % n == 0)


def nearest_steps(size):
    return sorted(range(1, size), key=lambda k: (min(k, size - k), k))


class Grid:
    def __init__(self):
        self.total = lax.axis_size("expert")
        self.sizes = split_axis(self.total)
        self.me = lax.axis_index("expert")
        _, nb, nc = self.sizes
        self.pos = (self.me // (nb * nc), (self.me // nc) % nb, self.me % nc)
        self.parts = lax.axis_size("tensor")
        self.part = lax.axis_index("tensor")

    def flat(self, a, b, c):
        _, nb, nc = self.sizes
        return (a * nb + b) * nc + c

    def shift(self, value, axis, step):
        pairs = []
        for a in range(self.sizes[0]):
            for b in range(self.sizes[1]):
                for c in range(self.sizes[2]):
                    src = [a, b, c]
                    src[axis] = (src[axis] + step) % self.sizes[axis]
                    pairs.append((self.flat(*src), self.flat(a, b, c)))
        return lax.ppermute(value, "expert", pairs)

    def tensor_shift(self, value, step):
        n = self.parts
        return lax.ppermute(value, "tensor", [((i + step) % n, i) for i in range(n)])

    def ids(self):
        na, nb, nc = self.sizes
        a, b, c = self.pos
        places = [(da, db, dc) for dc in range(nc) for db in range(nb) for da in range(na)]
        return jnp.stack(
            [self.flat((a + da) % na, (b + db) % nb, (c + dc) % nc) for da, db, dc in places]
        ).astype(jnp.int32)

    def gather_small(self, own):
        out = own[None]
        for axis in range(3):
            parts = [out]
            for k in range(1, self.sizes[axis]):
                parts.append(self.shift(out, axis, k))
            out = jnp.concatenate(parts)
        return out

    def nearest(self):
        return nearest_steps(self.sizes[0])

    def gather(self, own, together=False):
        na, nb, nc = self.sizes
        line = {0: own}
        for k in self.nearest():
            line[k] = self.shift(own, 0, k)
        plane = [line[k] for k in range(na)]
        for j in range(1, nb):
            for k in range(na):
                plane.append(self.shift(line[k], 1, j))
        out = list(plane)
        for d in range(1, nc):
            for piece in [jnp.stack(plane)] if together else plane:
                out.append(self.shift(piece, 2, d))
        return out

    def gather_rows(self, own, lent):
        na, nb, nc = self.sizes
        width = own.shape[1]
        keep = width - (self.parts - 1) * lent
        mine = lax.dynamic_slice_in_dim(own, self.part * lent, keep, 1)
        lend = self.part * ((width - lent) // (self.parts - 1) - lent)
        plane = [(0, None, own)]
        swaps = [(0, None, own)]
        line = {}
        for k in self.nearest():
            line[k] = self.shift(mine, 0, k)
        for j in range(1, nb):
            piece = self.shift(own, 1, j)
            plane.append((j * na, None, piece))
            swaps.append((j * na, None, piece))
        for j in range(nb):
            row = dict(line)
            if j > 0:
                for k in self.nearest():
                    row[k] = self.shift(line[k], 1, j)
            kinds = [row]
            for h in range(1, self.parts):
                lent_row = {}
                for k in self.nearest():
                    piece = row[k]
                    if lent < keep:
                        piece = lax.dynamic_slice_in_dim(piece, lend, lent, 1)
                    lent_row[k] = self.tensor_shift(piece, h)
                kinds.append(lent_row)
            for h, pieces in enumerate(kinds):
                plane += [(j * na + k, h, pieces[k]) for k in range(1, na)]
                group = jnp.concatenate([pieces[k] for k in range(1, na)])
                swaps.append((j * na + 1, h, group))
        out = list(plane)
        for d in range(1, nc):
            for block, h, piece in swaps:
                out.append((d * na * nb + block, h, self.shift(piece, 2, d)))
        return out


def row_copies(where, at_ref, piece_refs, whole, sem, parts, tok):
    width = whole.shape[1]
    copies = []
    for n, ((block, h), ref) in enumerate(zip(where, piece_refs)):
        rows = pl.ds(block * tok, ref.shape[0])
        if h is None:
            to = whole.at[rows, :]
        else:
            cols = ref.shape[1]
            step = (width - cols) // (parts - 1)
            start = pl.multiple_of(((at_ref[0] + h) % parts) * step, LANES)
            to = whole.at[rows, pl.ds(start, cols)]
        copies.append(pltpu.make_async_copy(ref, to, sem.at[n]))
    return copies


def products(weight_refs, weights, acc, wsem, copies, whole, window_copy):
    steps, block = weights.shape[1:3]

    def fetch(i, j):
        rows = pl.ds(pl.multiple_of(j * block, LANES), block)
        return pltpu.make_async_copy(weight_refs[i].at[rows, :], weights.at[i, j], wsem.at[i, j])

    ahead = min(2, steps)
    for copy in copies:
        copy.start()
    for j in range(ahead):
        for i in range(len(weight_refs)):
            fetch(i, j).start()
    for copy in copies:
        copy.wait()

    def step(j, carry):
        @pl.when(j + ahead < steps)
        def _():
            for i in range(len(weight_refs)):
                fetch(i, j + ahead).start()

        rows = whole[:, pl.ds(pl.multiple_of(j * block, LANES), block)]
        for i in range(len(weight_refs)):
            fetch(i, j).wait()
            part = jnp.dot(rows, weights[i, j], preferred_element_type=F32)

            @pl.when(j == 0)
            def _(i=i, part=part):
                acc[i] = part

            @pl.when(j > 0)
            def _(i=i, part=part):
                acc[i] += part

        return carry

    lax.fori_loop(0, steps, step, 0)
    window_copy.start()


def pick_matrix(place, rows):
    ids = lax.broadcasted_iota(jnp.int32, (rows, place.shape[1]), 0)
    return jnp.where(ids == place, 1.0, 0.0).astype(BF)


def window_of(width, depth):
    return min(width, -(-(depth + LANES - 1) // LANES) * LANES)


def gate_kernel(where, parts, tok, at_ref, wg_ref, wu_ref, gate_ref, place_ref, *refs):
    count = len(where)
    pieces = refs[:count]
    proj_ref, up_ref, down_ref, window_ref, whole, weights, acc, sem, wsem, osem = refs[count:]
    start = pl.multiple_of(at_ref[1], LANES)
    window = pltpu.make_async_copy(
        whole.at[:, pl.ds(start, window_ref.shape[1])], window_ref, osem.at[0]
    )
    copies = row_copies(where, at_ref, pieces, whole, sem, parts, tok)
    products([wg_ref, wu_ref], weights, acc, wsem, copies, whole, window)
    outs = [
        pltpu.make_async_copy(acc.at[0], proj_ref, osem.at[1]),
        pltpu.make_async_copy(acc.at[1], up_ref, osem.at[2]),
    ]
    for copy in outs:
        copy.start()
    proj = acc[0]
    hidden = proj * jax.nn.sigmoid(proj) * acc[1]
    weighted = (gate_ref[...] * hidden).astype(BF)
    pick = pick_matrix(place_ref[...], down_ref.shape[0])
    down_ref[...] = jnp.dot(pick, weighted, preferred_element_type=F32).astype(BF)
    for copy in [window] + outs:
        copy.wait()


def down_kernel(where, parts, tok, at_ref, wd_ref, gate_ref, place_ref, proj_ref, up_ref, *refs):
    count = len(where)
    pieces = refs[:count]
    pre_ref, upg_ref, pre_rows_ref, upg_rows_ref, score_ref, window_ref = refs[count : count + 6]
    whole, weights, acc, sem, wsem, osem = refs[count + 6 :]
    start = pl.multiple_of(at_ref[1], LANES)
    window = pltpu.make_async_copy(
        whole.at[:, pl.ds(start, window_ref.shape[1])], window_ref, osem.at[0]
    )
    copies = row_copies(where, at_ref, pieces, whole, sem, parts, tok)
    products([wd_ref], weights, acc, wsem, copies, whole, window)
    proj, up, dy_down = proj_ref[...], up_ref[...], acc[0]
    sigma = jax.nn.sigmoid(proj)
    activated = proj * sigma
    score = jnp.sum(activated * up * dy_down, axis=1, keepdims=True)
    lane = lax.broadcasted_iota(jnp.int32, score_ref.shape, 1)
    score_ref[...] = jnp.where(lane == at_ref[2], score, 0.0).astype(BF)
    grad = gate_ref[...] * dy_down
    upg = (grad * activated).astype(BF)
    pre = (grad * up * sigma * (1.0 + proj * (1.0 - sigma))).astype(BF)
    pre_ref[...] = pre
    upg_ref[...] = upg
    pick = pick_matrix(place_ref[...], pre_rows_ref.shape[0])
    pre_rows_ref[...] = jnp.dot(pick, pre, preferred_element_type=F32).astype(BF)
    upg_rows_ref[...] = jnp.dot(pick, upg, preferred_element_type=F32).astype(BF)
    window.wait()


def full(shape):
    return pl.BlockSpec(shape, lambda *_: (0,) * len(shape))


def forward_call(kernel, at, weights, small, pieces, outs, far, width, rows_all, depth, parts, tok):
    where = [(block, h) for block, h, _ in pieces]
    values = [piece for _, _, piece in pieces]
    hidden = weights[0].shape[1]
    block = block_of(width, 1792)
    steps = width // block
    window = window_of(width, depth)
    body = lambda *refs: kernel(where, parts, tok, *refs)
    return pl.pallas_call(
        body,
        grid_spec=pltpu.PrefetchScalarGridSpec(
            num_scalar_prefetch=1,
            grid=(1,),
            in_specs=[ANY for _ in weights]
            + [full(value.shape) for value in small]
            + [ANY for _ in values],
            out_specs=[ANY] * far + [full(out.shape) for out in outs[far:]] + [ANY],
            scratch_shapes=[
                pltpu.VMEM((rows_all, width), BF),
                pltpu.VMEM((len(weights), steps, block, hidden), BF),
                pltpu.VMEM((len(weights), rows_all, hidden), F32),
                pltpu.SemaphoreType.DMA((len(values),)),
                pltpu.SemaphoreType.DMA((len(weights), steps)),
                pltpu.SemaphoreType.DMA((1 + far,)),
            ],
        ),
        out_shape=list(outs) + [jax.ShapeDtypeStruct((rows_all, window), BF)],
    )(at, *weights, *small, *values)


def input_kernel(index_ref, pre_ref, up_ref, score_ref, wg_ref, wu_ref, out_ref, weights, obuf, wsem, osem):
    dims = (((1,), (1,)), ((), ()))
    cores, rows, _ = out_ref.shape
    steps, block = weights.shape[1:3]
    part = steps * block
    wide = score_ref.shape[1]

    def fetch(i, j):
        at = pl.ds(pl.multiple_of(index_ref[0] * part + j * block, LANES), block)
        return pltpu.make_async_copy((wg_ref, wu_ref)[i].at[at, :], weights.at[i, j], wsem.at[i, j])

    def put(c, j):
        cols = pl.ds(pl.multiple_of(j * block, LANES), block)
        return pltpu.make_async_copy(obuf.at[j, c], out_ref.at[c, :, cols], osem.at[c, j])

    def put_score(c):
        return pltpu.make_async_copy(
            score_ref.at[pl.ds(c * rows, rows), :],
            out_ref.at[c, :, pl.ds(part, wide)],
            osem.at[c, steps],
        )

    for j in range(steps):
        for i in range(2):
            fetch(i, j).start()
    for c in range(cores):
        put_score(c).start()

    def step(j, carry):
        fetch(0, j).wait()
        fetch(1, j).wait()
        acc = lax.dot_general(pre_ref[...], weights[0, j], dims, preferred_element_type=F32)
        acc = acc + lax.dot_general(up_ref[...], weights[1, j], dims, preferred_element_type=F32)
        for c in range(cores):
            obuf[j, c] = acc[c * rows : (c + 1) * rows].astype(BF)
            put(c, j).start()
        return carry

    lax.fori_loop(0, steps, step, 0)
    for c in range(cores):
        put_score(c).wait()
        for j in range(steps):
            put(c, j).wait()


def input_part(grid, h, pre, up, score, w_gate, w_up):
    tokens, hidden = pre.shape
    width = w_gate.shape[0]
    parts, cores = grid.parts, grid.sizes[2]
    part = width // parts
    block = block_of(part, 512)
    steps = part // block
    index = ((grid.part + h) % parts).astype(jnp.int32).reshape(1)
    rows = tokens // cores
    return pl.pallas_call(
        input_kernel,
        grid_spec=pltpu.PrefetchScalarGridSpec(
            num_scalar_prefetch=1,
            grid=(1,),
            in_specs=[full((tokens, hidden)), full((tokens, hidden)), full(score.shape), ANY, ANY],
            out_specs=ANY,
            scratch_shapes=[
                pltpu.VMEM((2, steps, block, hidden), BF),
                pltpu.VMEM((steps, cores, rows, block), BF),
                pltpu.SemaphoreType.DMA((2, steps)),
                pltpu.SemaphoreType.DMA((cores, steps + 1)),
            ],
        ),
        out_shape=jax.ShapeDtypeStruct((cores, rows, part + LANES), BF),
    )(index, pre, up, score, w_gate, w_up)


def pick_kernel(place_ref, both_ref, xo_ref, dyo_ref):
    per, depth, rows = xo_ref.shape
    dims = (((1,), (1,)), ((), ()))
    for n in range(per):
        pick = pick_matrix(place_ref[n], rows)
        both = lax.dot_general(both_ref[...], pick, dims, preferred_element_type=F32).astype(BF)
        xo_ref[n] = both[:depth]
        dyo_ref[n] = both[depth:]


def picked(place, x_t, dy_t, rows):
    slots, tokens = place.shape
    depth = x_t.shape[0]
    per = 4 if slots % 4 == 0 else 1
    out = jax.ShapeDtypeStruct((slots, depth, rows), BF)
    both = jnp.concatenate([x_t, dy_t])
    return pl.pallas_call(
        pick_kernel,
        grid=(slots // per,),
        in_specs=[pl.BlockSpec((per, 1, tokens), lambda s: (s, 0, 0)), full(both.shape)],
        out_specs=[pl.BlockSpec((per, depth, rows), lambda s: (s, 0, 0))] * 2,
        out_shape=[out, out],
    )(place.reshape(slots, 1, tokens), both)


def expert_kernel(slots, replicas, first, table_ref, rows_ref, *refs):
    pieces = []
    for ref in refs:
        if len(pieces) < slots:
            pieces += [ref] if len(ref.shape) == 2 else [ref.at[n] for n in range(ref.shape[0])]
    out_ref, left, right, obuf, sem_l, sem_r, osem = refs[-7:]
    experts = slots - replicas

    def left_copy(i):
        return pltpu.make_async_copy(rows_ref.at[i], left.at[i], sem_l.at[i])

    def right_copy(i, at):
        return pltpu.make_async_copy(pieces[i], right.at[at], sem_r.at[at])

    def put(e):
        return pltpu.make_async_copy(obuf.at[e], out_ref.at[e, first], osem.at[e])

    def issue(n, carry):
        i = table_ref[jnp.where(n < replicas, experts + n, n - replicas)]
        left_copy(i).start()
        for k in range(slots):

            @pl.when(i == k)
            def _(k=k):
                right_copy(k, k).start()

        return carry

    lax.fori_loop(0, slots, issue, 0)
    for r in range(replicas):
        i = table_ref[experts + r]
        left_copy(i).wait()
        right_copy(0, i).wait()

    def step(e, carry):
        at = table_ref[e]
        left_copy(at).wait()
        right_copy(0, at).wait()
        owned = table_ref[slots] == e
        for r in range(1, replicas):
            owned = jnp.logical_or(owned, table_ref[slots + r] == e)
        value = jnp.dot(left[at], right[at], preferred_element_type=F32)

        @pl.when(jnp.logical_not(owned))
        def _():
            obuf[e] = value.astype(BF)

        @pl.when(owned)
        def _():
            total = value
            for r in range(replicas):
                i = table_ref[experts + r]
                more = jnp.dot(left[i], right[i], preferred_element_type=F32)
                total = total + jnp.where(table_ref[slots + r] == e, more, 0.0)
            obuf[e] = total.astype(BF)

        put(e).start()
        return carry

    lax.fori_loop(0, experts, step, 0)

    def finish(e, carry):
        put(e).wait()
        return carry

    lax.fori_loop(0, experts, finish, 0)


def expert_sums(table, rows, pieces, first, total, previous, replicas):
    slots, depth, n = rows.shape
    experts = slots - replicas
    hidden = pieces[0].shape[-1]
    operands = [rows] + list(pieces)
    aliases = {}
    if previous is not None:
        operands.append(previous)
        aliases = {len(operands): 0}
    return pl.pallas_call(
        lambda *refs: expert_kernel(slots, replicas, first, *refs),
        grid_spec=pltpu.PrefetchScalarGridSpec(
            num_scalar_prefetch=1,
            grid=(1,),
            in_specs=[ANY for _ in operands],
            out_specs=ANY,
            scratch_shapes=[
                pltpu.VMEM((slots, depth, n), BF),
                pltpu.VMEM((slots, n, hidden), BF),
                pltpu.VMEM((experts, depth, hidden), BF),
                pltpu.SemaphoreType.DMA((slots,)),
                pltpu.SemaphoreType.DMA((slots,)),
                pltpu.SemaphoreType.DMA((experts,)),
            ],
        ),
        out_shape=jax.ShapeDtypeStruct((experts, total, depth, hidden), BF),
        input_output_aliases=aliases,
    )(table, *operands)


def lent_columns(width, parts, sevenths):
    if parts > 2:
        return width // parts
    return width * sevenths // 7 // LANES * LANES


def after(value, *others):
    return lax.optimization_barrier((value, *others))[0]


def per_device(tokens, cotangent, gate_weights, route_slots, replica_owner, w_gate, w_up, w_down):
    grid = Grid()
    slots = grid.total
    na, nb, nc = grid.sizes
    tok, width = tokens.shape
    top = route_slots.shape[1]
    rows = tok * top * 3 // 2
    replicas = replica_owner.shape[0]
    wg, wu, wd = w_gate[0], w_up[0], w_down[0]
    hidden = wg.shape[1]
    all_tok = tok * slots
    depth = width // slots
    part = width // grid.parts

    meta = jnp.concatenate(
        [route_slots.astype(BF), gate_weights, jnp.zeros((tok, LANES - 2 * top), BF)], axis=1
    )
    meta_all = grid.gather_small(meta).reshape(all_tok, LANES)
    x_pieces = grid.gather_rows(tokens, width // grid.parts)
    dy_pieces = grid.gather_rows(cotangent, lent_columns(width, grid.parts, 2))

    ids = grid.ids()
    routes = meta_all[:, :top].astype(jnp.int32)
    gates = meta_all[:, top : 2 * top].astype(F32)
    token_ids = (ids[:, None] * tok + jnp.arange(tok, dtype=jnp.int32)[None, :]).reshape(-1)
    named = jnp.any(routes[None, :, :] == ids[:, None, None], axis=2)
    before = (token_ids[:, None] < token_ids[None, :]).astype(BF)
    place = jnp.dot(named.astype(BF), before, preferred_element_type=F32).astype(jnp.int32)
    place = jnp.where(named, place, -1)
    gate = jnp.sum(jnp.where(routes == ids[0], gates, 0.0), axis=1)[:, None]

    first = grid.me * depth
    window = window_of(width, depth)
    start = jnp.minimum(first // LANES * LANES, width - window)
    at = jnp.stack([grid.part, start, grid.me]).astype(jnp.int32)
    square = jax.ShapeDtypeStruct((all_tok, hidden), F32)
    square_b = jax.ShapeDtypeStruct((all_tok, hidden), BF)
    proj, up_proj, down, x_window = forward_call(
        gate_kernel,
        at,
        [wg, wu],
        [gate, place[:1]],
        x_pieces,
        [square, square, jax.ShapeDtypeStruct((rows, hidden), BF)],
        2,
        width,
        all_tok,
        depth,
        grid.parts,
        tok,
    )
    down_all = grid.gather(down, together=True)
    pre, upg, pre_rows, upg_rows, score, dy_window = forward_call(
        down_kernel,
        at,
        [wd],
        [gate, place[:1], proj, up_proj],
        dy_pieces,
        [
            square_b,
            square_b,
            jax.ShapeDtypeStruct((rows, hidden), BF),
            jax.ShapeDtypeStruct((rows, hidden), BF),
            jax.ShapeDtypeStruct((all_tok, LANES), BF),
        ],
        0,
        width,
        all_tok,
        depth,
        grid.parts,
        tok,
    )
    pre_all = grid.gather(pre_rows)
    upg_all = grid.gather(upg_rows)

    terms = {}
    for h in [*range(1, grid.parts), 0]:
        share = input_part(grid, h, pre, upg, score, wg, wu)
        total = share[0].astype(F32)
        for k in range(1, nc):
            total = total + grid.shift(share[k], 2, -k).astype(F32)
        terms[h] = total.astype(BF)
        if h > 0:
            terms[h] = grid.tensor_shift(terms[h], -h)
    terms = [terms[h] for h in range(grid.parts)]
    if grid.parts > 2:
        terms = list(jnp.roll(jnp.stack(terms)[::-1], grid.part + 1, axis=0))
    total = terms[0].astype(F32)
    for term in terms[1:]:
        total = total + term.astype(F32)
    total = total.astype(BF).reshape(nb, na, tok, part + LANES)
    half = part // 2 // LANES * LANES
    left, right = total[..., :half], total[..., half:]
    left_line, right_line = left[0].astype(F32), right[:, 0].astype(F32)
    for k in nearest_steps(na):
        right_line = right_line + grid.shift(right[:, k], 0, -k).astype(F32)
    for k in range(1, nb):
        left_line = left_line + grid.shift(left[k], 1, -k).astype(F32)
    left_line, right_line = left_line.astype(BF), right_line.astype(BF)
    left_sum, right_sum = left_line[0].astype(F32), right_line[0].astype(F32)
    for k in nearest_steps(na):
        left_sum = left_sum + grid.shift(left_line[k], 0, -k).astype(F32)
    for k in range(1, nb):
        right_sum = right_sum + grid.shift(right_line[k], 1, -k).astype(F32)
    last = jnp.concatenate([left_sum, right_sum], axis=1)
    input_grads = last[:, :part].astype(BF)
    lane = jnp.arange(LANES, dtype=jnp.int32)
    own_routes = route_slots[:, :, None] == lane[None, None, :]
    gate_grads = jnp.sum(jnp.where(own_routes, last[:, None, part:], 0.0), axis=2).astype(BF)

    x_window, dy_window = after(x_window, share), after(dy_window, share)
    x_t = lax.dynamic_slice_in_dim(x_window, first - start, depth, 1).T
    dy_t = lax.dynamic_slice_in_dim(dy_window, first - start, depth, 1).T
    spot = jnp.sum(
        jnp.where(
            ids[None, :] == jnp.arange(slots, dtype=jnp.int32)[:, None],
            jnp.arange(slots, dtype=jnp.int32)[None, :],
            0,
        ),
        axis=1,
    )
    x_pick, dy_pick = picked(place, x_t, dy_t, rows)
    table = jnp.concatenate([spot, replica_owner]).astype(jnp.int32)
    out = expert_sums(table, dy_pick, down_all, 2, 3, None, replicas)
    out = expert_sums(table, x_pick, pre_all, 0, 3, out, replicas)
    out = expert_sums(table, x_pick, upg_all, 1, 3, out, replicas)
    return input_grads, gate_grads, jnp.transpose(out, (0, 2, 1, 3))


def solution(mesh):
    in_specs = (
        P("expert", None),
        P("expert", None),
        P("expert", None),
        P("expert", None),
        P(),
        P("expert", None, "tensor"),
        P("expert", None, "tensor"),
        P("expert", None, "tensor"),
    )
    out_specs = (P("expert", "tensor"), P("expert", None), P(None, "expert", None, "tensor"))

    return jax.shard_map(
        per_device, mesh=mesh, in_specs=in_specs, out_specs=out_specs, check_vma=False
    )
```

```python
import jax
import jax.numpy as jnp
from jax import lax
from jax.experimental import pallas as pl
from jax.experimental.pallas import tpu as pltpu
from jax.sharding import PartitionSpec as P


BF = jnp.bfloat16
F32 = jnp.float32
LANES = 128
ANY = pl.BlockSpec(memory_space=pl.ANY)


def split_axis(total):
    cores = 2
    chips = total // cores
    b = 1
    while b * b * 4 <= chips:
        b *= 2
    return chips // b, b, cores


def block_of(size, most):
    return max(n for n in range(LANES, most + 1, LANES) if size % n == 0)


def nearest_steps(size):
    return sorted(range(1, size), key=lambda k: (min(k, size - k), k))


class Grid:
    def __init__(self):
        self.total = lax.axis_size("expert")
        self.sizes = split_axis(self.total)
        self.me = lax.axis_index("expert")
        _, nb, nc = self.sizes
        self.pos = (self.me // (nb * nc), (self.me // nc) % nb, self.me % nc)
        self.parts = lax.axis_size("tensor")
        self.part = lax.axis_index("tensor")

    def flat(self, a, b, c):
        _, nb, nc = self.sizes
        return (a * nb + b) * nc + c

    def shift(self, value, axis, step):
        pairs = []
        for a in range(self.sizes[0]):
            for b in range(self.sizes[1]):
                for c in range(self.sizes[2]):
                    src = [a, b, c]
                    src[axis] = (src[axis] + step) % self.sizes[axis]
                    pairs.append((self.flat(*src), self.flat(a, b, c)))
        return lax.ppermute(value, "expert", pairs)

    def tensor_shift(self, value, step):
        n = self.parts
        return lax.ppermute(value, "tensor", [((i + step) % n, i) for i in range(n)])

    def ids(self):
        na, nb, nc = self.sizes
        a, b, c = self.pos
        places = [(da, db, dc) for dc in range(nc) for db in range(nb) for da in range(na)]
        return jnp.stack(
            [self.flat((a + da) % na, (b + db) % nb, (c + dc) % nc) for da, db, dc in places]
        ).astype(jnp.int32)

    def gather_small(self, own):
        out = own[None]
        for axis in range(3):
            parts = [out]
            for k in range(1, self.sizes[axis]):
                parts.append(self.shift(out, axis, k))
            out = jnp.concatenate(parts)
        return out

    def nearest(self):
        return nearest_steps(self.sizes[0])

    def gather(self, own, together=False):
        na, nb, nc = self.sizes
        line = {0: own}
        for k in self.nearest():
            line[k] = self.shift(own, 0, k)
        plane = [line[k] for k in range(na)]
        for j in range(1, nb):
            for k in range(na):
                plane.append(self.shift(line[k], 1, j))
        out = list(plane)
        for d in range(1, nc):
            for piece in [jnp.stack(plane)] if together else plane:
                out.append(self.shift(piece, 2, d))
        return out

    def gather_rows(self, own, lent, turn=()):
        na, nb, nc = self.sizes
        width = own.shape[1]
        keep = width - (self.parts - 1) * lent
        mine = lax.dynamic_slice_in_dim(own, self.part * lent, keep, 1)
        lend = self.part * ((width - lent) // (self.parts - 1) - lent)
        plane = [(0, None, own)]
        swaps = [(0, None, own)]
        line = {}
        for k in self.nearest():
            line[k] = self.shift(mine, 0, k)
        for j in range(1, nb):
            piece = self.shift(own, 1, j)
            plane.append((j * na, None, piece))
            swaps.append((j * na, None, piece))
        for j in range(nb):
            row = dict(line)
            if j > 0:
                for k in self.nearest():
                    row[k] = self.shift(line[k], 1, j)
            kinds = [row]
            for h in range(1, self.parts):
                lent_row = {}
                for k in self.nearest():
                    piece = row[k]
                    if lent < keep:
                        piece = lax.dynamic_slice_in_dim(piece, lend, lent, 1)
                    if j > 0 and k in turn:
                        lent_row[k] = self.shift(lent_rows[h][k], 1, j)
                    else:
                        lent_row[k] = self.tensor_shift(piece, h)
                kinds.append(lent_row)
            if j == 0:
                lent_rows = kinds
            for h, pieces in enumerate(kinds):
                plane += [(j * na + k, h, pieces[k]) for k in range(1, na)]
                group = jnp.concatenate([pieces[k] for k in range(1, na)])
                swaps.append((j * na + 1, h, group))
        out = list(plane)
        for d in range(1, nc):
            for block, h, piece in swaps:
                out.append((d * na * nb + block, h, self.shift(piece, 2, d)))
        return out


def row_copies(where, at_ref, piece_refs, whole, sem, parts, tok):
    width = whole.shape[1]
    copies = []
    for n, ((block, h), ref) in enumerate(zip(where, piece_refs)):
        rows = pl.ds(block * tok, ref.shape[0])
        if h is None:
            to = whole.at[rows, :]
        else:
            cols = ref.shape[1]
            step = (width - cols) // (parts - 1)
            start = pl.multiple_of(((at_ref[0] + h) % parts) * step, LANES)
            to = whole.at[rows, pl.ds(start, cols)]
        copies.append(pltpu.make_async_copy(ref, to, sem.at[n]))
    return copies


def products(weight_refs, weights, acc, wsem, copies, whole, window_copy):
    steps, block = weights.shape[1:3]

    def fetch(i, j):
        rows = pl.ds(pl.multiple_of(j * block, LANES), block)
        return pltpu.make_async_copy(weight_refs[i].at[rows, :], weights.at[i, j], wsem.at[i, j])

    ahead = min(2, steps)
    for copy in copies:
        copy.start()
    for j in range(ahead):
        for i in range(len(weight_refs)):
            fetch(i, j).start()
    for copy in copies:
        copy.wait()

    def step(j, carry):
        @pl.when(j + ahead < steps)
        def _():
            for i in range(len(weight_refs)):
                fetch(i, j + ahead).start()

        rows = whole[:, pl.ds(pl.multiple_of(j * block, LANES), block)]
        for i in range(len(weight_refs)):
            fetch(i, j).wait()
            part = jnp.dot(rows, weights[i, j], preferred_element_type=F32)

            @pl.when(j == 0)
            def _(i=i, part=part):
                acc[i] = part

            @pl.when(j > 0)
            def _(i=i, part=part):
                acc[i] += part

        return carry

    lax.fori_loop(0, steps, step, 0)
    window_copy.start()


def pick_matrix(place, rows):
    ids = lax.broadcasted_iota(jnp.int32, (rows, place.shape[1]), 0)
    return jnp.where(ids == place, 1.0, 0.0).astype(BF)


def window_of(width, depth):
    return min(width, -(-(depth + LANES - 1) // LANES) * LANES)


def gate_kernel(where, parts, tok, at_ref, wg_ref, wu_ref, gate_ref, place_ref, *refs):
    count = len(where)
    pieces = refs[:count]
    proj_ref, up_ref, down_ref, window_ref, whole, weights, acc, sem, wsem, osem = refs[count:]
    start = pl.multiple_of(at_ref[1], LANES)
    window = pltpu.make_async_copy(
        whole.at[:, pl.ds(start, window_ref.shape[1])], window_ref, osem.at[0]
    )
    copies = row_copies(where, at_ref, pieces, whole, sem, parts, tok)
    products([wg_ref, wu_ref], weights, acc, wsem, copies, whole, window)
    outs = [
        pltpu.make_async_copy(acc.at[0], proj_ref, osem.at[1]),
        pltpu.make_async_copy(acc.at[1], up_ref, osem.at[2]),
    ]
    for copy in outs:
        copy.start()
    proj = acc[0]
    hidden = proj * jax.nn.sigmoid(proj) * acc[1]
    weighted = (gate_ref[...] * hidden).astype(BF)
    pick = pick_matrix(place_ref[...], down_ref.shape[0])
    down_ref[...] = jnp.dot(pick, weighted, preferred_element_type=F32).astype(BF)
    for copy in [window] + outs:
        copy.wait()


def down_kernel(where, parts, tok, at_ref, wd_ref, gate_ref, place_ref, proj_ref, up_ref, *refs):
    count = len(where)
    pieces = refs[:count]
    pre_ref, upg_ref, pre_rows_ref, upg_rows_ref, score_ref, window_ref = refs[count : count + 6]
    whole, weights, acc, sem, wsem, osem = refs[count + 6 :]
    start = pl.multiple_of(at_ref[1], LANES)
    window = pltpu.make_async_copy(
        whole.at[:, pl.ds(start, window_ref.shape[1])], window_ref, osem.at[0]
    )
    copies = row_copies(where, at_ref, pieces, whole, sem, parts, tok)
    products([wd_ref], weights, acc, wsem, copies, whole, window)
    proj, up, dy_down = proj_ref[...], up_ref[...], acc[0]
    sigma = jax.nn.sigmoid(proj)
    activated = proj * sigma
    score = jnp.sum(activated * up * dy_down, axis=1, keepdims=True)
    lane = lax.broadcasted_iota(jnp.int32, score_ref.shape, 1)
    score_ref[...] = jnp.where(lane == at_ref[2], score, 0.0).astype(BF)
    grad = gate_ref[...] * dy_down
    upg = (grad * activated).astype(BF)
    pre = (grad * up * sigma * (1.0 + proj * (1.0 - sigma))).astype(BF)
    pre_ref[...] = pre
    upg_ref[...] = upg
    pick = pick_matrix(place_ref[...], pre_rows_ref.shape[0])
    pre_rows_ref[...] = jnp.dot(pick, pre, preferred_element_type=F32).astype(BF)
    upg_rows_ref[...] = jnp.dot(pick, upg, preferred_element_type=F32).astype(BF)
    window.wait()


def full(shape):
    return pl.BlockSpec(shape, lambda *_: (0,) * len(shape))


def forward_call(kernel, at, weights, small, pieces, outs, far, width, rows_all, depth, parts, tok):
    where = [(block, h) for block, h, _ in pieces]
    values = [piece for _, _, piece in pieces]
    hidden = weights[0].shape[1]
    block = block_of(width, 1792)
    steps = width // block
    window = window_of(width, depth)
    body = lambda *refs: kernel(where, parts, tok, *refs)
    return pl.pallas_call(
        body,
        grid_spec=pltpu.PrefetchScalarGridSpec(
            num_scalar_prefetch=1,
            grid=(1,),
            in_specs=[ANY for _ in weights]
            + [full(value.shape) for value in small]
            + [ANY for _ in values],
            out_specs=[ANY] * far + [full(out.shape) for out in outs[far:]] + [ANY],
            scratch_shapes=[
                pltpu.VMEM((rows_all, width), BF),
                pltpu.VMEM((len(weights), steps, block, hidden), BF),
                pltpu.VMEM((len(weights), rows_all, hidden), F32),
                pltpu.SemaphoreType.DMA((len(values),)),
                pltpu.SemaphoreType.DMA((len(weights), steps)),
                pltpu.SemaphoreType.DMA((1 + far,)),
            ],
        ),
        out_shape=list(outs) + [jax.ShapeDtypeStruct((rows_all, window), BF)],
    )(at, *weights, *small, *values)


def input_kernel(index_ref, pre_ref, up_ref, score_ref, wg_ref, wu_ref, *refs):
    dims = (((1,), (1,)), ((), ()))
    *out_refs, weights, obuf, wsem, osem = refs
    steps, cores, rows, block = obuf.shape
    part = steps * block
    wide = score_ref.shape[1]

    def fetch(i, j):
        at = pl.ds(pl.multiple_of(index_ref[0] * part + j * block, LANES), block)
        return pltpu.make_async_copy((wg_ref, wu_ref)[i].at[at, :], weights.at[i, j], wsem.at[i, j])

    def put(c, j):
        cols = pl.ds(pl.multiple_of(j * block, LANES), block)
        return pltpu.make_async_copy(obuf.at[j, c], out_refs[c].at[:, cols], osem.at[c, j])

    def put_score(c):
        return pltpu.make_async_copy(
            score_ref.at[pl.ds(c * rows, rows), :],
            out_refs[c].at[:, pl.ds(part, wide)],
            osem.at[c, steps],
        )

    for j in range(steps):
        for i in range(2):
            fetch(i, j).start()
    for c in range(cores):
        put_score(c).start()

    def step(j, carry):
        fetch(0, j).wait()
        fetch(1, j).wait()
        acc = lax.dot_general(pre_ref[...], weights[0, j], dims, preferred_element_type=F32)
        acc = acc + lax.dot_general(up_ref[...], weights[1, j], dims, preferred_element_type=F32)
        for c in range(cores):
            obuf[j, c] = acc[c * rows : (c + 1) * rows].astype(BF)
            put(c, j).start()
        return carry

    lax.fori_loop(0, steps, step, 0)
    for c in range(cores):
        put_score(c).wait()
        for j in range(steps):
            put(c, j).wait()


def input_part(grid, h, pre, up, score, w_gate, w_up):
    tokens, hidden = pre.shape
    width = w_gate.shape[0]
    parts, cores = grid.parts, grid.sizes[2]
    part = width // parts
    block = block_of(part, 512)
    steps = part // block
    index = ((grid.part + h) % parts).astype(jnp.int32).reshape(1)
    rows = tokens // cores
    return pl.pallas_call(
        input_kernel,
        grid_spec=pltpu.PrefetchScalarGridSpec(
            num_scalar_prefetch=1,
            grid=(1,),
            in_specs=[full((tokens, hidden)), full((tokens, hidden)), full(score.shape), ANY, ANY],
            out_specs=[ANY] * cores,
            scratch_shapes=[
                pltpu.VMEM((2, steps, block, hidden), BF),
                pltpu.VMEM((steps, cores, rows, block), BF),
                pltpu.SemaphoreType.DMA((2, steps)),
                pltpu.SemaphoreType.DMA((cores, steps + 1)),
            ],
        ),
        out_shape=[jax.ShapeDtypeStruct((rows, part + LANES), BF)] * cores,
    )(index, pre, up, score, w_gate, w_up)


def pick_kernel(place_ref, features_ref, out_ref):
    dims = (((1,), (1,)), ((), ()))
    for n in range(out_ref.shape[0]):
        pick = pick_matrix(place_ref[n], out_ref.shape[2])
        out_ref[n] = lax.dot_general(
            features_ref[...], pick, dims, preferred_element_type=F32
        ).astype(BF)


def picked(place, features, rows):
    slots, tokens = place.shape
    depth = features.shape[0]
    per = 4 if slots % 4 == 0 else 1
    return pl.pallas_call(
        pick_kernel,
        grid=(slots // per,),
        in_specs=[pl.BlockSpec((per, 1, tokens), lambda s: (s, 0, 0)), full(features.shape)],
        out_specs=pl.BlockSpec((per, depth, rows), lambda s: (s, 0, 0)),
        out_shape=jax.ShapeDtypeStruct((slots, depth, rows), BF),
    )(place.reshape(slots, 1, tokens), features)


def expert_kernel(slots, replicas, first, table_ref, rows_ref, *refs):
    pieces = []
    for ref in refs:
        if len(pieces) < slots:
            pieces += [ref] if len(ref.shape) == 2 else [ref.at[n] for n in range(ref.shape[0])]
    out_ref, left, right, obuf, sem_l, sem_r, osem = refs[-7:]
    experts = slots - replicas

    def left_copy(i):
        return pltpu.make_async_copy(rows_ref.at[i], left.at[i], sem_l.at[i])

    def right_copy(i, at):
        return pltpu.make_async_copy(pieces[i], right.at[at], sem_r.at[at])

    def put(e):
        return pltpu.make_async_copy(obuf.at[e], out_ref.at[e, first], osem.at[e])

    def issue(n, carry):
        i = table_ref[jnp.where(n < replicas, experts + n, n - replicas)]
        left_copy(i).start()
        for k in range(slots):

            @pl.when(i == k)
            def _(k=k):
                right_copy(k, k).start()

        return carry

    lax.fori_loop(0, slots, issue, 0)
    for r in range(replicas):
        i = table_ref[experts + r]
        left_copy(i).wait()
        right_copy(0, i).wait()

    def step(e, carry):
        at = table_ref[e]
        left_copy(at).wait()
        right_copy(0, at).wait()
        owned = table_ref[slots] == e
        for r in range(1, replicas):
            owned = jnp.logical_or(owned, table_ref[slots + r] == e)
        value = jnp.dot(left[at], right[at], preferred_element_type=F32)

        @pl.when(jnp.logical_not(owned))
        def _():
            obuf[e] = value.astype(BF)

        @pl.when(owned)
        def _():
            total = value
            for r in range(replicas):
                i = table_ref[experts + r]
                more = jnp.dot(left[i], right[i], preferred_element_type=F32)
                total = total + jnp.where(table_ref[slots + r] == e, more, 0.0)
            obuf[e] = total.astype(BF)

        put(e).start()
        return carry

    lax.fori_loop(0, experts, step, 0)

    def finish(e, carry):
        put(e).wait()
        return carry

    lax.fori_loop(0, experts, finish, 0)


def expert_sums(table, rows, pieces, first, total, previous, replicas):
    slots, depth, n = rows.shape
    experts = slots - replicas
    hidden = pieces[0].shape[-1]
    operands = [rows] + list(pieces)
    aliases = {}
    if previous is not None:
        operands.append(previous)
        aliases = {len(operands): 0}
    return pl.pallas_call(
        lambda *refs: expert_kernel(slots, replicas, first, *refs),
        grid_spec=pltpu.PrefetchScalarGridSpec(
            num_scalar_prefetch=1,
            grid=(1,),
            in_specs=[ANY for _ in operands],
            out_specs=ANY,
            scratch_shapes=[
                pltpu.VMEM((slots, depth, n), BF),
                pltpu.VMEM((slots, n, hidden), BF),
                pltpu.VMEM((experts, depth, hidden), BF),
                pltpu.SemaphoreType.DMA((slots,)),
                pltpu.SemaphoreType.DMA((slots,)),
                pltpu.SemaphoreType.DMA((experts,)),
            ],
        ),
        out_shape=jax.ShapeDtypeStruct((experts, total, depth, hidden), BF),
        input_output_aliases=aliases,
    )(table, *operands)


def after(value, *others):
    return lax.optimization_barrier((value, *others))[0]


def per_device(tokens, cotangent, gate_weights, route_slots, replica_owner, w_gate, w_up, w_down):
    grid = Grid()
    slots = grid.total
    na, nb, nc = grid.sizes
    tok, width = tokens.shape
    top = route_slots.shape[1]
    rows = tok * top * 3 // 2
    replicas = replica_owner.shape[0]
    wg, wu, wd = w_gate[0], w_up[0], w_down[0]
    hidden = wg.shape[1]
    all_tok = tok * slots
    depth = width // slots
    part = width // grid.parts

    meta = jnp.concatenate(
        [route_slots.astype(BF), gate_weights, jnp.zeros((tok, LANES - 2 * top), BF)], axis=1
    )
    meta_all = grid.gather_small(meta).reshape(all_tok, LANES)
    x_pieces = grid.gather_rows(tokens, width // grid.parts)
    dy_pieces = grid.gather_rows(cotangent, width // grid.parts, grid.nearest()[-1:])

    ids = grid.ids()
    routes = meta_all[:, :top].astype(jnp.int32)
    gates = meta_all[:, top : 2 * top].astype(F32)
    token_ids = (ids[:, None] * tok + jnp.arange(tok, dtype=jnp.int32)[None, :]).reshape(-1)
    named = jnp.any(routes[None, :, :] == ids[:, None, None], axis=2)
    before = (token_ids[:, None] < token_ids[None, :]).astype(BF)
    place = jnp.dot(named.astype(BF), before, preferred_element_type=F32).astype(jnp.int32)
    place = jnp.where(named, place, -1)
    gate = jnp.sum(jnp.where(routes == ids[0], gates, 0.0), axis=1)[:, None]

    first = grid.me * depth
    window = window_of(width, depth)
    start = jnp.minimum(first // LANES * LANES, width - window)
    at = jnp.stack([grid.part, start, grid.me]).astype(jnp.int32)
    square = jax.ShapeDtypeStruct((all_tok, hidden), F32)
    square_b = jax.ShapeDtypeStruct((all_tok, hidden), BF)
    proj, up_proj, down, x_window = forward_call(
        gate_kernel,
        at,
        [wg, wu],
        [gate, place[:1]],
        x_pieces,
        [square, square, jax.ShapeDtypeStruct((rows, hidden), BF)],
        2,
        width,
        all_tok,
        depth,
        grid.parts,
        tok,
    )
    down_all = grid.gather(down)
    pre, upg, pre_rows, upg_rows, score, dy_window = forward_call(
        down_kernel,
        at,
        [wd],
        [gate, place[:1], proj, up_proj],
        dy_pieces,
        [
            square_b,
            square_b,
            jax.ShapeDtypeStruct((rows, hidden), BF),
            jax.ShapeDtypeStruct((rows, hidden), BF),
            jax.ShapeDtypeStruct((all_tok, LANES), BF),
        ],
        0,
        width,
        all_tok,
        depth,
        grid.parts,
        tok,
    )
    pre_all = grid.gather(pre_rows)
    upg_all = grid.gather(upg_rows)

    terms = {}
    for h in [*range(1, grid.parts), 0]:
        share = shares = input_part(grid, h, pre, upg, score, wg, wu)
        total = share[0].astype(F32)
        for k in range(1, nc):
            total = total + grid.shift(share[k], 2, -k).astype(F32)
        terms[h] = total.astype(BF)
        if h > 0:
            terms[h] = grid.tensor_shift(terms[h], -h)
    terms = [terms[h] for h in range(grid.parts)]
    if grid.parts > 2:
        terms = list(jnp.roll(jnp.stack(terms)[::-1], grid.part + 1, axis=0))
    total = terms[0].astype(F32)
    for term in terms[1:]:
        total = total + term.astype(F32)
    total = total.astype(BF).reshape(nb, na, tok, part + LANES)
    half = part // 2 // LANES * LANES
    left, right = total[..., :half], total[..., half:]
    left_line, right_line = left[0].astype(F32), right[:, 0].astype(F32)
    for k in nearest_steps(na):
        right_line = right_line + grid.shift(right[:, k], 0, -k).astype(F32)
    for k in range(1, nb):
        left_line = left_line + grid.shift(left[k], 1, -k).astype(F32)
    left_line, right_line = left_line.astype(BF), right_line.astype(BF)
    left_sum, right_sum = left_line[0].astype(F32), right_line[0].astype(F32)
    for k in nearest_steps(na):
        left_sum = left_sum + grid.shift(left_line[k], 0, -k).astype(F32)
    for k in range(1, nb):
        right_sum = right_sum + grid.shift(right_line[k], 1, -k).astype(F32)
    last = jnp.concatenate([left_sum, right_sum], axis=1)
    input_grads = last[:, :part].astype(BF)
    lane = jnp.arange(LANES, dtype=jnp.int32)
    own_routes = route_slots[:, :, None] == lane[None, None, :]
    gate_grads = jnp.sum(jnp.where(own_routes, last[:, None, part:], 0.0), axis=2).astype(BF)

    dy_window = after(dy_window, *shares)
    x_t = lax.dynamic_slice_in_dim(x_window, first - start, depth, 1).T
    dy_t = lax.dynamic_slice_in_dim(dy_window, first - start, depth, 1).T
    spot = jnp.sum(
        jnp.where(
            ids[None, :] == jnp.arange(slots, dtype=jnp.int32)[:, None],
            jnp.arange(slots, dtype=jnp.int32)[None, :],
            0,
        ),
        axis=1,
    )
    x_pick = picked(place, x_t, rows)
    dy_pick = picked(place, dy_t, rows)
    table = jnp.concatenate([spot, replica_owner]).astype(jnp.int32)
    out = expert_sums(table, dy_pick, down_all, 2, 3, None, replicas)
    out = expert_sums(table, x_pick, pre_all, 0, 3, out, replicas)
    out = expert_sums(table, x_pick, upg_all, 1, 3, out, replicas)
    return input_grads, gate_grads, jnp.transpose(out, (0, 2, 1, 3))


def solution(mesh):
    in_specs = (
        P("expert", None),
        P("expert", None),
        P("expert", None),
        P("expert", None),
        P(),
        P("expert", None, "tensor"),
        P("expert", None, "tensor"),
        P("expert", None, "tensor"),
    )
    out_specs = (P("expert", "tensor"), P("expert", None), P(None, "expert", None, "tensor"))

    return jax.shard_map(
        per_device, mesh=mesh, in_specs=in_specs, out_specs=out_specs, check_vma=False
    )
```

```python
import jax
import jax.numpy as jnp
from jax import lax
from jax.experimental import pallas as pl
from jax.experimental.pallas import tpu as pltpu
from jax.sharding import PartitionSpec as P


BF = jnp.bfloat16
F32 = jnp.float32
LANES = 128
ANY = pl.BlockSpec(memory_space=pl.ANY)


def split_axis(total):
    cores = 2
    chips = total // cores
    b = 1
    while b * b * 4 <= chips:
        b *= 2
    return chips // b, b, cores


def block_of(size, most):
    return max(n for n in range(LANES, most + 1, LANES) if size % n == 0)


def nearest_steps(size):
    return sorted(range(1, size), key=lambda k: (min(k, size - k), k))


class Grid:
    def __init__(self):
        self.total = lax.axis_size("expert")
        self.sizes = split_axis(self.total)
        self.me = lax.axis_index("expert")
        _, nb, nc = self.sizes
        self.pos = (self.me // (nb * nc), (self.me // nc) % nb, self.me % nc)
        self.parts = lax.axis_size("tensor")
        self.part = lax.axis_index("tensor")

    def flat(self, a, b, c):
        _, nb, nc = self.sizes
        return (a * nb + b) * nc + c

    def shift(self, value, axis, step):
        pairs = []
        for a in range(self.sizes[0]):
            for b in range(self.sizes[1]):
                for c in range(self.sizes[2]):
                    src = [a, b, c]
                    src[axis] = (src[axis] + step) % self.sizes[axis]
                    pairs.append((self.flat(*src), self.flat(a, b, c)))
        return lax.ppermute(value, "expert", pairs)

    def tensor_shift(self, value, step):
        n = self.parts
        return lax.ppermute(value, "tensor", [((i + step) % n, i) for i in range(n)])

    def ids(self):
        na, nb, nc = self.sizes
        a, b, c = self.pos
        places = [(da, db, dc) for dc in range(nc) for db in range(nb) for da in range(na)]
        return jnp.stack(
            [self.flat((a + da) % na, (b + db) % nb, (c + dc) % nc) for da, db, dc in places]
        ).astype(jnp.int32)

    def gather_small(self, own):
        out = own[None]
        for axis in range(3):
            parts = [out]
            for k in range(1, self.sizes[axis]):
                parts.append(self.shift(out, axis, k))
            out = jnp.concatenate(parts)
        return out

    def nearest(self):
        return nearest_steps(self.sizes[0])

    def gather(self, own, together=False):
        na, nb, nc = self.sizes
        line = {0: own}
        for k in self.nearest():
            line[k] = self.shift(own, 0, k)
        plane = [line[k] for k in range(na)]
        for j in range(1, nb):
            for k in range(na):
                plane.append(self.shift(line[k], 1, j))
        out = list(plane)
        for d in range(1, nc):
            for piece in [jnp.stack(plane)] if together else plane:
                out.append(self.shift(piece, 2, d))
        return out

    def gather_rows(self, own, lent, turn=()):
        na, nb, nc = self.sizes
        width = own.shape[1]
        keep = width - (self.parts - 1) * lent
        mine = lax.dynamic_slice_in_dim(own, self.part * lent, keep, 1)
        lend = self.part * ((width - lent) // (self.parts - 1) - lent)
        plane = [(0, None, own)]
        swaps = [(0, None, own)]
        line = {}
        for k in self.nearest():
            line[k] = self.shift(mine, 0, k)
        for j in range(1, nb):
            piece = self.shift(own, 1, j)
            plane.append((j * na, None, piece))
            swaps.append((j * na, None, piece))
        for j in range(nb):
            row = dict(line)
            if j > 0:
                for k in self.nearest():
                    row[k] = self.shift(line[k], 1, j)
            kinds = [row]
            for h in range(1, self.parts):
                lent_row = {}
                for k in self.nearest():
                    piece = row[k]
                    if lent < keep:
                        piece = lax.dynamic_slice_in_dim(piece, lend, lent, 1)
                    if j > 0 and k in turn:
                        lent_row[k] = self.shift(lent_rows[h][k], 1, j)
                    else:
                        lent_row[k] = self.tensor_shift(piece, h)
                kinds.append(lent_row)
            if j == 0:
                lent_rows = kinds
            for h, pieces in enumerate(kinds):
                plane += [(j * na + k, h, pieces[k]) for k in range(1, na)]
                group = jnp.concatenate([pieces[k] for k in range(1, na)])
                swaps.append((j * na + 1, h, group))
        out = list(plane)
        for d in range(1, nc):
            for block, h, piece in swaps:
                out.append((d * na * nb + block, h, self.shift(piece, 2, d)))
        return out


def row_copies(where, at_ref, piece_refs, whole, sem, parts, tok):
    width = whole.shape[1]
    copies = []
    for n, ((block, h), ref) in enumerate(zip(where, piece_refs)):
        rows = pl.ds(block * tok, ref.shape[0])
        if h is None:
            to = whole.at[rows, :]
        else:
            cols = ref.shape[1]
            step = (width - cols) // (parts - 1)
            start = pl.multiple_of(((at_ref[0] + h) % parts) * step, LANES)
            to = whole.at[rows, pl.ds(start, cols)]
        copies.append(pltpu.make_async_copy(ref, to, sem.at[n]))
    return copies


def products(weight_refs, weights, acc, wsem, copies, whole, window_copy):
    steps, block = weights.shape[1:3]

    def fetch(i, j):
        rows = pl.ds(pl.multiple_of(j * block, LANES), block)
        return pltpu.make_async_copy(weight_refs[i].at[rows, :], weights.at[i, j], wsem.at[i, j])

    ahead = min(2, steps)
    for copy in copies:
        copy.start()
    for j in range(ahead):
        for i in range(len(weight_refs)):
            fetch(i, j).start()
    for copy in copies:
        copy.wait()

    def step(j, carry):
        @pl.when(j + ahead < steps)
        def _():
            for i in range(len(weight_refs)):
                fetch(i, j + ahead).start()

        rows = whole[:, pl.ds(pl.multiple_of(j * block, LANES), block)]
        for i in range(len(weight_refs)):
            fetch(i, j).wait()
            part = jnp.dot(rows, weights[i, j], preferred_element_type=F32)

            @pl.when(j == 0)
            def _(i=i, part=part):
                acc[i] = part

            @pl.when(j > 0)
            def _(i=i, part=part):
                acc[i] += part

        return carry

    lax.fori_loop(0, steps, step, 0)
    window_copy.start()


def pick_matrix(place, rows):
    ids = lax.broadcasted_iota(jnp.int32, (rows, place.shape[1]), 0)
    return jnp.where(ids == place, 1.0, 0.0).astype(BF)


def window_of(width, depth):
    return min(width, -(-(depth + LANES - 1) // LANES) * LANES)


def gate_kernel(where, parts, tok, at_ref, wg_ref, wu_ref, gate_ref, place_ref, *refs):
    count = len(where)
    pieces = refs[:count]
    proj_ref, up_ref, down_ref, window_ref, whole, weights, acc, sem, wsem, osem = refs[count:]
    start = pl.multiple_of(at_ref[1], LANES)
    window = pltpu.make_async_copy(
        whole.at[:, pl.ds(start, window_ref.shape[1])], window_ref, osem.at[0]
    )
    copies = row_copies(where, at_ref, pieces, whole, sem, parts, tok)
    products([wg_ref, wu_ref], weights, acc, wsem, copies, whole, window)
    outs = [
        pltpu.make_async_copy(acc.at[0], proj_ref, osem.at[1]),
        pltpu.make_async_copy(acc.at[1], up_ref, osem.at[2]),
    ]
    for copy in outs:
        copy.start()
    proj = acc[0]
    hidden = proj * jax.nn.sigmoid(proj) * acc[1]
    weighted = (gate_ref[...] * hidden).astype(BF)
    pick = pick_matrix(place_ref[...], down_ref.shape[0])
    down_ref[...] = jnp.dot(pick, weighted, preferred_element_type=F32).astype(BF)
    for copy in [window] + outs:
        copy.wait()


def down_kernel(where, parts, tok, at_ref, wd_ref, gate_ref, place_ref, proj_ref, up_ref, *refs):
    count = len(where)
    pieces = refs[:count]
    pre_ref, upg_ref, pre_rows_ref, upg_rows_ref, score_ref, window_ref = refs[count : count + 6]
    whole, weights, acc, sem, wsem, osem = refs[count + 6 :]
    start = pl.multiple_of(at_ref[1], LANES)
    window = pltpu.make_async_copy(
        whole.at[:, pl.ds(start, window_ref.shape[1])], window_ref, osem.at[0]
    )
    copies = row_copies(where, at_ref, pieces, whole, sem, parts, tok)
    products([wd_ref], weights, acc, wsem, copies, whole, window)
    proj, up, dy_down = proj_ref[...], up_ref[...], acc[0]
    sigma = jax.nn.sigmoid(proj)
    activated = proj * sigma
    score = jnp.sum(activated * up * dy_down, axis=1, keepdims=True)
    lane = lax.broadcasted_iota(jnp.int32, score_ref.shape, 1)
    score_ref[...] = jnp.where(lane == at_ref[2], score, 0.0).astype(BF)
    grad = gate_ref[...] * dy_down
    upg = (grad * activated).astype(BF)
    pre = (grad * up * sigma * (1.0 + proj * (1.0 - sigma))).astype(BF)
    pre_ref[...] = pre
    upg_ref[...] = upg
    pick = pick_matrix(place_ref[...], pre_rows_ref.shape[0])
    pre_rows_ref[...] = jnp.dot(pick, pre, preferred_element_type=F32).astype(BF)
    upg_rows_ref[...] = jnp.dot(pick, upg, preferred_element_type=F32).astype(BF)
    window.wait()


def full(shape):
    return pl.BlockSpec(shape, lambda *_: (0,) * len(shape))


def forward_call(kernel, at, weights, small, pieces, outs, far, width, rows_all, depth, parts, tok):
    where = [(block, h) for block, h, _ in pieces]
    values = [piece for _, _, piece in pieces]
    hidden = weights[0].shape[1]
    block = block_of(width, 1792)
    steps = width // block
    window = window_of(width, depth)
    body = lambda *refs: kernel(where, parts, tok, *refs)
    return pl.pallas_call(
        body,
        grid_spec=pltpu.PrefetchScalarGridSpec(
            num_scalar_prefetch=1,
            grid=(1,),
            in_specs=[ANY for _ in weights]
            + [full(value.shape) for value in small]
            + [ANY for _ in values],
            out_specs=[ANY] * far + [full(out.shape) for out in outs[far:]] + [ANY],
            scratch_shapes=[
                pltpu.VMEM((rows_all, width), BF),
                pltpu.VMEM((len(weights), steps, block, hidden), BF),
                pltpu.VMEM((len(weights), rows_all, hidden), F32),
                pltpu.SemaphoreType.DMA((len(values),)),
                pltpu.SemaphoreType.DMA((len(weights), steps)),
                pltpu.SemaphoreType.DMA((1 + far,)),
            ],
        ),
        out_shape=list(outs) + [jax.ShapeDtypeStruct((rows_all, window), BF)],
    )(at, *weights, *small, *values)


def input_kernel(index_ref, pre_ref, up_ref, score_ref, wg_ref, wu_ref, *refs):
    dims = (((1,), (1,)), ((), ()))
    *out_refs, weights, obuf, wsem, osem = refs
    steps, cores, rows, block = obuf.shape
    part = steps * block
    wide = score_ref.shape[1]

    def fetch(i, j):
        at = pl.ds(pl.multiple_of(index_ref[0] * part + j * block, LANES), block)
        return pltpu.make_async_copy((wg_ref, wu_ref)[i].at[at, :], weights.at[i, j], wsem.at[i, j])

    def put(c, j):
        cols = pl.ds(pl.multiple_of(j * block, LANES), block)
        return pltpu.make_async_copy(obuf.at[j, c], out_refs[c].at[:, cols], osem.at[c, j])

    def put_score(c):
        return pltpu.make_async_copy(
            score_ref.at[pl.ds(c * rows, rows), :],
            out_refs[c].at[:, pl.ds(part, wide)],
            osem.at[c, steps],
        )

    for j in range(steps):
        for i in range(2):
            fetch(i, j).start()
    for c in range(cores):
        put_score(c).start()

    def step(j, carry):
        fetch(0, j).wait()
        fetch(1, j).wait()
        acc = lax.dot_general(pre_ref[...], weights[0, j], dims, preferred_element_type=F32)
        acc = acc + lax.dot_general(up_ref[...], weights[1, j], dims, preferred_element_type=F32)
        for c in range(cores):
            obuf[j, c] = acc[c * rows : (c + 1) * rows].astype(BF)
            put(c, j).start()
        return carry

    lax.fori_loop(0, steps, step, 0)
    for c in range(cores):
        put_score(c).wait()
        for j in range(steps):
            put(c, j).wait()


def input_part(grid, h, pre, up, score, w_gate, w_up):
    tokens, hidden = pre.shape
    width = w_gate.shape[0]
    parts, cores = grid.parts, grid.sizes[2]
    part = width // parts
    block = block_of(part, 512)
    steps = part // block
    index = ((grid.part + h) % parts).astype(jnp.int32).reshape(1)
    rows = tokens // cores
    return pl.pallas_call(
        input_kernel,
        grid_spec=pltpu.PrefetchScalarGridSpec(
            num_scalar_prefetch=1,
            grid=(1,),
            in_specs=[full((tokens, hidden)), full((tokens, hidden)), full(score.shape), ANY, ANY],
            out_specs=[ANY] * cores,
            scratch_shapes=[
                pltpu.VMEM((2, steps, block, hidden), BF),
                pltpu.VMEM((steps, cores, rows, block), BF),
                pltpu.SemaphoreType.DMA((2, steps)),
                pltpu.SemaphoreType.DMA((cores, steps + 1)),
            ],
        ),
        out_shape=[jax.ShapeDtypeStruct((rows, part + LANES), BF)] * cores,
    )(index, pre, up, score, w_gate, w_up)


def pick_kernel(place_ref, features_ref, out_ref):
    dims = (((1,), (1,)), ((), ()))
    for n in range(out_ref.shape[0]):
        pick = pick_matrix(place_ref[n], out_ref.shape[2])
        out_ref[n] = lax.dot_general(
            features_ref[...], pick, dims, preferred_element_type=F32
        ).astype(BF)


def picked(place, features, rows):
    slots, tokens = place.shape
    depth = features.shape[0]
    per = 4 if slots % 4 == 0 else 1
    return pl.pallas_call(
        pick_kernel,
        grid=(slots // per,),
        in_specs=[pl.BlockSpec((per, 1, tokens), lambda s: (s, 0, 0)), full(features.shape)],
        out_specs=pl.BlockSpec((per, depth, rows), lambda s: (s, 0, 0)),
        out_shape=jax.ShapeDtypeStruct((slots, depth, rows), BF),
    )(place.reshape(slots, 1, tokens), features)


def expert_kernel(slots, replicas, first, table_ref, rows_ref, *refs):
    pieces = []
    for ref in refs:
        if len(pieces) < slots:
            pieces += [ref] if len(ref.shape) == 2 else [ref.at[n] for n in range(ref.shape[0])]
    out_ref, left, right, obuf, sem_l, sem_r, osem = refs[-7:]
    experts = slots - replicas

    def left_copy(i):
        return pltpu.make_async_copy(rows_ref.at[i], left.at[i], sem_l.at[i])

    def right_copy(i, at):
        return pltpu.make_async_copy(pieces[i], right.at[at], sem_r.at[at])

    def put(e):
        return pltpu.make_async_copy(obuf.at[e], out_ref.at[e, first], osem.at[e])

    def issue(n, carry):
        i = table_ref[jnp.where(n < replicas, experts + n, n - replicas)]
        left_copy(i).start()
        for k in range(slots):

            @pl.when(i == k)
            def _(k=k):
                right_copy(k, k).start()

        return carry

    lax.fori_loop(0, slots, issue, 0)
    for r in range(replicas):
        i = table_ref[experts + r]
        left_copy(i).wait()
        right_copy(0, i).wait()

    def step(e, carry):
        at = table_ref[e]
        left_copy(at).wait()
        right_copy(0, at).wait()
        owned = table_ref[slots] == e
        for r in range(1, replicas):
            owned = jnp.logical_or(owned, table_ref[slots + r] == e)
        value = jnp.dot(left[at], right[at], preferred_element_type=F32)

        @pl.when(jnp.logical_not(owned))
        def _():
            obuf[e] = value.astype(BF)

        @pl.when(owned)
        def _():
            total = value
            for r in range(replicas):
                i = table_ref[experts + r]
                more = jnp.dot(left[i], right[i], preferred_element_type=F32)
                total = total + jnp.where(table_ref[slots + r] == e, more, 0.0)
            obuf[e] = total.astype(BF)

        put(e).start()
        return carry

    lax.fori_loop(0, experts, step, 0)

    def finish(e, carry):
        put(e).wait()
        return carry

    lax.fori_loop(0, experts, finish, 0)


def expert_sums(table, rows, pieces, first, total, previous, replicas):
    slots, depth, n = rows.shape
    experts = slots - replicas
    hidden = pieces[0].shape[-1]
    operands = [rows] + list(pieces)
    aliases = {}
    if previous is not None:
        operands.append(previous)
        aliases = {len(operands): 0}
    return pl.pallas_call(
        lambda *refs: expert_kernel(slots, replicas, first, *refs),
        grid_spec=pltpu.PrefetchScalarGridSpec(
            num_scalar_prefetch=1,
            grid=(1,),
            in_specs=[ANY for _ in operands],
            out_specs=ANY,
            scratch_shapes=[
                pltpu.VMEM((slots, depth, n), BF),
                pltpu.VMEM((slots, n, hidden), BF),
                pltpu.VMEM((experts, depth, hidden), BF),
                pltpu.SemaphoreType.DMA((slots,)),
                pltpu.SemaphoreType.DMA((slots,)),
                pltpu.SemaphoreType.DMA((experts,)),
            ],
        ),
        out_shape=jax.ShapeDtypeStruct((experts, total, depth, hidden), BF),
        input_output_aliases=aliases,
    )(table, *operands)


def after(value, *others):
    return lax.optimization_barrier((value, *others))[0]


def per_device(tokens, cotangent, gate_weights, route_slots, replica_owner, w_gate, w_up, w_down):
    grid = Grid()
    slots = grid.total
    na, nb, nc = grid.sizes
    tok, width = tokens.shape
    top = route_slots.shape[1]
    rows = tok * top * 3 // 2
    replicas = replica_owner.shape[0]
    wg, wu, wd = w_gate[0], w_up[0], w_down[0]
    hidden = wg.shape[1]
    all_tok = tok * slots
    depth = width // slots
    part = width // grid.parts

    meta = jnp.concatenate(
        [route_slots.astype(BF), gate_weights, jnp.zeros((tok, LANES - 2 * top), BF)], axis=1
    )
    meta_all = grid.gather_small(meta).reshape(all_tok, LANES)
    x_pieces = grid.gather_rows(tokens, width // grid.parts)
    dy_pieces = grid.gather_rows(cotangent, width // grid.parts, grid.nearest()[-1:])

    ids = grid.ids()
    routes = meta_all[:, :top].astype(jnp.int32)
    gates = meta_all[:, top : 2 * top].astype(F32)
    token_ids = (ids[:, None] * tok + jnp.arange(tok, dtype=jnp.int32)[None, :]).reshape(-1)
    named = jnp.any(routes[None, :, :] == ids[:, None, None], axis=2)
    before = (token_ids[:, None] < token_ids[None, :]).astype(BF)
    place = jnp.dot(named.astype(BF), before, preferred_element_type=F32).astype(jnp.int32)
    place = jnp.where(named, place, -1)
    gate = jnp.sum(jnp.where(routes == ids[0], gates, 0.0), axis=1)[:, None]

    first = grid.me * depth
    window = window_of(width, depth)
    start = jnp.minimum(first // LANES * LANES, width - window)
    at = jnp.stack([grid.part, start, grid.me]).astype(jnp.int32)
    square = jax.ShapeDtypeStruct((all_tok, hidden), F32)
    square_b = jax.ShapeDtypeStruct((all_tok, hidden), BF)
    proj, up_proj, down, x_window = forward_call(
        gate_kernel,
        at,
        [wg, wu],
        [gate, place[:1]],
        x_pieces,
        [square, square, jax.ShapeDtypeStruct((rows, hidden), BF)],
        2,
        width,
        all_tok,
        depth,
        grid.parts,
        tok,
    )
    down_all = grid.gather(down)
    pre, upg, pre_rows, upg_rows, score, dy_window = forward_call(
        down_kernel,
        at,
        [wd],
        [gate, place[:1], proj, up_proj],
        dy_pieces,
        [
            square_b,
            square_b,
            jax.ShapeDtypeStruct((rows, hidden), BF),
            jax.ShapeDtypeStruct((rows, hidden), BF),
            jax.ShapeDtypeStruct((all_tok, LANES), BF),
        ],
        0,
        width,
        all_tok,
        depth,
        grid.parts,
        tok,
    )
    pre_all = grid.gather(pre_rows)
    upg_all = grid.gather(upg_rows)

    terms = {}
    for h in [*range(1, grid.parts), 0]:
        share = shares = input_part(grid, h, pre, upg, score, wg, wu)
        total = share[0].astype(F32)
        for k in range(1, nc):
            total = total + grid.shift(share[k], 2, -k).astype(F32)
        terms[h] = total.astype(BF)
        if h > 0:
            terms[h] = grid.tensor_shift(terms[h], -h)
    terms = [terms[h] for h in range(grid.parts)]
    if grid.parts > 2:
        terms = list(jnp.roll(jnp.stack(terms)[::-1], grid.part + 1, axis=0))
    total = terms[0].astype(F32)
    for term in terms[1:]:
        total = total + term.astype(F32)
    total = total.astype(BF).reshape(nb, na, tok, part + LANES)
    half = part // 2 // LANES * LANES
    left, right = total[..., :half], total[..., half:]
    left_line, right_line = left[0].astype(F32), right[:, 0].astype(F32)
    for k in nearest_steps(na):
        right_line = right_line + grid.shift(right[:, k], 0, -k).astype(F32)
    for k in range(1, nb):
        left_line = left_line + grid.shift(left[k], 1, -k).astype(F32)
    left_line, right_line = left_line.astype(BF), right_line.astype(BF)
    left_sum, right_sum = left_line[0].astype(F32), right_line[0].astype(F32)
    for k in nearest_steps(na):
        left_sum = left_sum + grid.shift(left_line[k], 0, -k).astype(F32)
    for k in range(1, nb):
        right_sum = right_sum + grid.shift(right_line[k], 1, -k).astype(F32)
    scores = right_sum[:, part - half :]
    input_grads = jnp.concatenate(
        [left_sum.astype(BF), right_sum[:, : part - half].astype(BF)], axis=1
    )
    lane = jnp.arange(LANES, dtype=jnp.int32)
    own_routes = route_slots[:, :, None] == lane[None, None, :]
    gate_grads = jnp.sum(jnp.where(own_routes, scores[:, None, :], 0.0), axis=2).astype(BF)

    dy_window = after(dy_window, *shares)
    x_t = lax.dynamic_slice_in_dim(x_window, first - start, depth, 1).T
    dy_t = lax.dynamic_slice_in_dim(dy_window, first - start, depth, 1).T
    spot = jnp.sum(
        jnp.where(
            ids[None, :] == jnp.arange(slots, dtype=jnp.int32)[:, None],
            jnp.arange(slots, dtype=jnp.int32)[None, :],
            0,
        ),
        axis=1,
    )
    x_pick = picked(place, x_t, rows)
    dy_pick = picked(place, dy_t, rows)
    table = jnp.concatenate([spot, replica_owner]).astype(jnp.int32)
    out = expert_sums(table, dy_pick, down_all, 2, 3, None, replicas)
    out = expert_sums(table, x_pick, pre_all, 0, 3, out, replicas)
    out = expert_sums(table, x_pick, upg_all, 1, 3, out, replicas)
    return input_grads, gate_grads, jnp.transpose(out, (0, 2, 1, 3))


def solution(mesh):
    in_specs = (
        P("expert", None),
        P("expert", None),
        P("expert", None),
        P("expert", None),
        P(),
        P("expert", None, "tensor"),
        P("expert", None, "tensor"),
        P("expert", None, "tensor"),
    )
    out_specs = (P("expert", "tensor"), P("expert", None), P(None, "expert", None, "tensor"))

    return jax.shard_map(
        per_device, mesh=mesh, in_specs=in_specs, out_specs=out_specs, check_vma=False
    )
```
